32 devices in a mesh: seq: 16 (over z, x, core), chan: 2 (over y).
Axes of the slice: x: 2, y: 2, z: 4, core: 2. Of those that a mesh axis runs over, the one named last changes fastest.
Arguments:
- inputs: bfloat16 [4096, 2048], P('chan', 'seq'), may hold values from -6 to 6
- gating: bfloat16 [4096, 2048], P('chan', 'seq'), may hold values from -6 to 6
- grad_out: bfloat16 [4096, 2048], P('chan', 'seq'), may hold values from -6 to 6
- filters: float32 [64, 2048], P(None, ('seq', 'chan')), as said below
Outputs:
- grad_inputs: bfloat16 [4096, 2048], P('chan', 'seq')
- grad_gating: bfloat16 [4096, 2048], P('chan', 'seq')
- grad_filters: float32 [64, 2048], P(None, ('seq', 'chan'))
The draws below stay inside these ranges and needn't reach their ends.
Inputs may be any that keep to these rules, and one draw needn't show every extreme that they name: `filters`: every entry's magnitude is at most 0.77 times the square root of 131072.
All inputs are finite; a program needn't handle non-finite values.
Results may differ from the reference program's by a relative error of at most 0.0049.
Values may be sent and summed in bfloat16 or wider, within the bound.
A program may use at most 64 MiB of HBM per device.

```python
import math
import jax
import jax.numpy as jnp
from jax import lax

D = 4096
G = 64
GROUP_WIDTH = 64
LENGTH_OF_TEXT = 2048


def draw_filters(key, part):
    keys = jax.random.split(key, 6)
    ordinal_locations = jnp.arange(LENGTH_OF_TEXT, dtype=jnp.float32)[None, :]
    slow_share = 0.5
    retained_mask = jax.random.bernoulli(keys[0], slow_share, (G, 1))
    gradual_decay = jnp.exp(jax.random.uniform(keys[1], (G, 1), minval=math.log(0.05), maxval=0.0)) / LENGTH_OF_TEXT
    quick_decay = jnp.exp(jax.random.uniform(keys[2], (G, 1), minval=math.log(1.0 / 50.0), maxval=math.log(1.0 / 30.0)))
    pulse_count_per_unit = jnp.where(retained_mask, gradual_decay, quick_decay)
    spots = jax.random.randint(keys[3], (G, 2), 0, LENGTH_OF_TEXT).astype(jnp.float32)
    masking_draws = jax.random.uniform(keys[4], (G, 2), minval=0.5, maxval=0.8)
    forwarded_signal = ordinal_locations[:, :, None] >= spots[:, None, :]
    pulse_groupings = jnp.prod(jnp.where(forwarded_signal, masking_draws[:, None, :], 1.0), axis=-1)
    power_level = (1.0 - jnp.exp(-2.0 * pulse_count_per_unit)) / (1.0 - jnp.exp(-2.0 * pulse_count_per_unit * LENGTH_OF_TEXT))
    sinusoid_peak = jnp.sqrt(power_level * (GROUP_WIDTH * LENGTH_OF_TEXT))
    jitter_offset = jnp.clip(jax.random.normal(keys[5], (G, LENGTH_OF_TEXT)), -3.0, 3.0)
    return (jitter_offset * sinusoid_peak * jnp.exp(-pulse_count_per_unit * ordinal_locations) * pulse_groupings).astype(jnp.float32)


def steps_of(stream_key, extent, shards, least, top_value):
    def one(axis_at, shards_of):
        draws = jax.random.uniform(jax.random.fold_in(jax.random.fold_in(stream_key, 6), axis_at), (shards_of,), jnp.float32, least / len(shards), top_value / len(shards))
        return jnp.repeat(jnp.exp(draws), extent[axis_at] // shards_of).reshape((-1,) + (1,) * (len(extent) - axis_at - 1))

    level = one(*shards[0])
    for cut in shards[1:]:
        level = level * one(*cut)
    return level


def scatter_about(own_key, shape, width, reach, pieces=(), held_as=jnp.bfloat16):
    array = width * jax.random.normal(own_key, shape, jnp.float32)
    if pieces:
        array = array * steps_of(own_key, shape, pieces, -0.22, 0.18)
    return jnp.clip(array, -reach, reach).astype(held_as)


def setup_inputs(seed: int = 0) -> dict:
    streams_of = jax.random.split(jax.random.key(seed), 5)
    inputs = scatter_about(streams_of[0], (D, LENGTH_OF_TEXT), 1.0, 6.0, ((0, 2), (1, 16)))
    gating = scatter_about(streams_of[1], (D, LENGTH_OF_TEXT), 1.0, 6.0, ((0, 2), (1, 16)))
    grad_out = scatter_about(streams_of[2], (D, LENGTH_OF_TEXT), 1.0, 6.0, ((0, 2), (1, 16)))
    filters = draw_filters(jax.random.fold_in(streams_of[4], 71), 0)
    return dict(inputs=inputs, gating=gating, grad_out=grad_out, filters=filters)


def reference(inputs, gating, grad_out, filters):
    factor = 1.0 / math.sqrt(GROUP_WIDTH * LENGTH_OF_TEXT)
    padded = 2 * LENGTH_OF_TEXT

    def per_group(operands):
        values, gate_part, upstream, kernel = operands
        product_b = lax.optimization_barrier((gate_part.astype(jnp.float32) * upstream.astype(jnp.float32)).astype(jnp.bfloat16))
        product = product_b.astype(jnp.float32)
        spec_in = jnp.fft.rfft(values.astype(jnp.float32), n=padded, axis=-1)
        spec_up = jnp.fft.rfft(product, n=padded, axis=-1)
        spec_ker = jnp.fft.rfft(kernel * factor, n=padded)
        convolved = jnp.fft.irfft(spec_in * spec_ker[None, :], n=padded, axis=-1)[:, :LENGTH_OF_TEXT]
        conv_b = lax.optimization_barrier(convolved.astype(jnp.bfloat16))
        grad_gate = (upstream.astype(jnp.float32) * conv_b.astype(jnp.float32)).astype(jnp.bfloat16)
        grad_input = jnp.fft.irfft(spec_up * jnp.conj(spec_ker)[None, :], n=padded, axis=-1)[:, :LENGTH_OF_TEXT]
        grad_kernel = factor * jnp.fft.irfft(lax.optimization_barrier(jnp.sum(jnp.conj(spec_in) * spec_up, axis=0)), n=padded)[:LENGTH_OF_TEXT]
        return (grad_input.astype(jnp.bfloat16), grad_gate, grad_kernel)
    shaped = (inputs.reshape(G, GROUP_WIDTH, LENGTH_OF_TEXT), gating.reshape(G, GROUP_WIDTH, LENGTH_OF_TEXT), grad_out.reshape(G, GROUP_WIDTH, LENGTH_OF_TEXT), filters)
    grad_input, grad_gate, grad_kernel = lax.map(per_group, shaped)
    return (grad_input.reshape(D, LENGTH_OF_TEXT), grad_gate.reshape(D, LENGTH_OF_TEXT), grad_kernel)
```

```python
import functools
import math

import jax
import jax.numpy as jnp
from jax import lax
from jax.experimental import pallas as pl
from jax.experimental.pallas import tpu as pltpu
from jax.sharding import PartitionSpec as P

D = 4096
G = 64


HIGHEST = lax.Precision.HIGHEST


def make_tables(seq_count, block_len):
    outer = 2 * seq_count
    total = outer * block_len
    outer_index = jnp.arange(outer, dtype=jnp.int32)
    block_index = jnp.arange(seq_count, dtype=jnp.int32)
    inner_index = jnp.arange(block_len, dtype=jnp.int32)
    block_angle = (outer_index[:, None] * block_index[None, :] % outer).astype(jnp.float32) * (
        2.0 * math.pi / outer
    )
    twist_angle = (outer_index[:, None] * inner_index[None, :] % total).astype(jnp.float32) * (
        2.0 * math.pi / total
    )
    inner_angle = (inner_index[:, None] * inner_index[None, :] % block_len).astype(jnp.float32) * (
        2.0 * math.pi / block_len
    )
    return (
        jnp.cos(block_angle),
        jnp.sin(block_angle),
        jnp.cos(twist_angle),
        jnp.sin(twist_angle),
        jnp.cos(inner_angle),
        jnp.sin(inner_angle),
    )


def right_product(values, table):
    return jnp.einsum("ckm,mj->ckj", values, table, precision=HIGHEST)


def forward_dft(signal, tables):
    block_cos, block_sin, twist_cos, twist_sin, inner_cos, inner_sin = tables
    real_first = jnp.einsum("kn,cnm->ckm", block_cos, signal, precision=HIGHEST)
    imag_first = -jnp.einsum("kn,cnm->ckm", block_sin, signal, precision=HIGHEST)
    real_twist = real_first * twist_cos + imag_first * twist_sin
    imag_twist = imag_first * twist_cos - real_first * twist_sin
    real_spec = right_product(real_twist, inner_cos) + right_product(imag_twist, inner_sin)
    imag_spec = right_product(imag_twist, inner_cos) - right_product(real_twist, inner_sin)
    return (real_spec, imag_spec)


def inverse_dft(real_spec, imag_spec, tables):
    block_cos, block_sin, twist_cos, twist_sin, inner_cos, inner_sin = tables
    real_first = right_product(real_spec, inner_cos) - right_product(imag_spec, inner_sin)
    imag_first = right_product(real_spec, inner_sin) + right_product(imag_spec, inner_cos)
    real_twist = real_first * twist_cos - imag_first * twist_sin
    imag_twist = real_first * twist_sin + imag_first * twist_cos
    total = real_spec.shape[1] * real_spec.shape[2]
    result = jnp.einsum("kn,ckm->cnm", block_cos, real_twist, precision=HIGHEST)
    result = result - jnp.einsum("kn,ckm->cnm", block_sin, imag_twist, precision=HIGHEST)
    return result / total


def shards(inputs, gating, grad_out, filters):
    seq_count = lax.axis_size("seq")
    chan_count = lax.axis_size("chan")
    chan_rows, block_len = inputs.shape
    local_chan = chan_rows // seq_count
    group_width = D // G
    groups_here = G // chan_count
    local_groups = max(1, local_chan // group_width)
    group_share = local_chan // local_groups
    copies = max(1, seq_count // groups_here)
    length = block_len * seq_count
    outer = 2 * seq_count
    factor = 1.0 / math.sqrt(group_width * length)
    tables = make_tables(seq_count, block_len)
    whole = lax.all_gather(filters, ("seq", "chan"), axis=1, tiled=True)
    first_group = (
        lax.axis_index("chan") * chan_rows + lax.axis_index("seq") * local_chan
    ) // group_width
    kernel_rows = lax.dynamic_slice_in_dim(whole, first_group, local_groups, 0)
    kernel_blocks = kernel_rows.reshape(local_groups, seq_count, block_len)
    kernel_real, kernel_imag = forward_dft(kernel_blocks * factor, tables)
    kernel_real = kernel_real[:, None]
    kernel_imag = kernel_imag[:, None]
    shaped_inputs = inputs.reshape(chan_rows, 1, block_len)
    values, gate_part, upstream = (
        lax.all_to_all(shaped_inputs, "seq", split_axis=0, concat_axis=1, tiled=True),
        lax.all_to_all(
            gating.reshape(chan_rows, 1, block_len), "seq", split_axis=0, concat_axis=1, tiled=True
        ),
        lax.all_to_all(
            grad_out.reshape(chan_rows, 1, block_len),
            "seq",
            split_axis=0,
            concat_axis=1,
            tiled=True,
        ),
    )
    input_real, input_imag = forward_dft(values.astype(jnp.float32), tables)
    upstream_f = upstream.astype(jnp.float32)
    product_b = lax.optimization_barrier(
        (gate_part.astype(jnp.float32) * upstream_f).astype(jnp.bfloat16)
    )
    up_real, up_imag = forward_dft(product_b.astype(jnp.float32), tables)
    grouped_shape = (local_groups, group_share, outer, block_len)
    input_real = input_real.reshape(grouped_shape)
    input_imag = input_imag.reshape(grouped_shape)
    up_real = up_real.reshape(grouped_shape)
    up_imag = up_imag.reshape(grouped_shape)
    flat_shape = (local_chan, outer, block_len)
    conv_real = input_real * kernel_real - input_imag * kernel_imag
    conv_imag = input_real * kernel_imag + input_imag * kernel_real
    convolved = inverse_dft(conv_real.reshape(flat_shape), conv_imag.reshape(flat_shape), tables)
    conv_b = convolved.astype(jnp.bfloat16)
    second = (upstream_f * lax.optimization_barrier(conv_b).astype(jnp.float32)).astype(
        jnp.bfloat16
    )
    back_real = up_real * kernel_real + up_imag * kernel_imag
    back_imag = up_imag * kernel_real - up_real * kernel_imag
    grad_input = inverse_dft(
        back_real.reshape(flat_shape), back_imag.reshape(flat_shape), tables
    ).astype(jnp.bfloat16)
    returned_input, returned_second = (
        lax.all_to_all(grad_input, "seq", split_axis=1, concat_axis=0, tiled=True),
        lax.all_to_all(second, "seq", split_axis=1, concat_axis=0, tiled=True),
    )
    returned_second = returned_second.reshape(chan_rows, block_len)
    cross_real = jnp.sum(input_real * up_real + input_imag * up_imag, axis=1)
    cross_imag = jnp.sum(input_real * up_imag - input_imag * up_real, axis=1)
    partial_grad = inverse_dft(cross_real, cross_imag, tables) * factor
    received = lax.all_to_all(partial_grad, "seq", split_axis=1, concat_axis=0, tiled=True)
    summed = received.reshape(groups_here, copies, block_len).sum(axis=1)
    grad_filters = lax.all_to_all(summed, "chan", split_axis=1, concat_axis=0, tiled=True)
    return (returned_input.reshape(chan_rows, block_len), returned_second, grad_filters)


GROUP_WIDTH = D // G
MESH = pl.DeviceIdType.MESH
TILE = 256
LAYERS = 4
DELAY_COMPUTE, DELAY_FINISH = 2, 4
SPLIT_LAG = 4
NT = (((1,), (1,)), ((), ()))
NN = (((1,), (0,)), ((), ()))


def dot(a, b, dims):
    return lax.dot_general(a, b, dims, preferred_element_type=jnp.float32)


def layered_kernel(
    seq_count,
    chan_count,
    x_hbm,
    gate_hbm,
    up_hbm,
    raw_hbm,
    gi_ref,
    gg_ref,
    grad_ref,
    gate_ref,
    up_ref,
    raw_ref,
    filt_ref,
    filt_in,
    filt_all,
    u_loc,
    xs,
    us,
    table,
    acc_c,
    acc_g,
    cv,
    gv,
    conv_in,
    held,
    part_out,
    part_in,
    fg_out,
    fg_layer,
    fg_sum,
    fg_in,
    load_sem,
    x_send,
    u_send,
    c_send,
    g_send,
    z_send,
    p_send,
    f_send,
    k_send,
    x_recv,
    u_recv,
    c_recv,
    g_recv,
    z_recv,
    p_recv,
    f_recv,
    fz_recv,
    k_recv,
    kz_recv,
):
    seq = lax.axis_index("seq")
    chan = lax.axis_index("chan")
    peers = seq_count // LAYERS
    crew = peers * chan_count
    layer = seq // peers
    spot = lax.rem(seq, peers)
    slot = spot * chan_count + chan
    last = LAYERS - 1
    groups = xs.shape[0]
    block = x_hbm.shape[1]
    per_tile = TILE // block
    length = block * seq_count
    tiles = length // TILE
    half = tiles // LAYERS
    width = GROUP_WIDTH
    layer_rows = half * width
    local_chan = groups * width
    share = raw_hbm.shape[1]
    factor = 1.0 / math.sqrt(width * length)

    loads = [
        pltpu.make_async_copy(gate_hbm, gate_ref, load_sem.at[0]),
        pltpu.make_async_copy(up_hbm, up_ref, load_sem.at[1]),
        pltpu.make_async_copy(raw_hbm, raw_ref, load_sem.at[2]),
    ]
    for load in loads:
        load.start()

    barrier = pltpu.get_barrier_semaphore()

    def greet(to_seq, to_chan):
        pl.semaphore_signal(barrier, inc=1, device_id=(to_seq, to_chan), device_id_type=MESH)

    def crew_member(k):
        other = lax.rem(slot + k, crew)
        return other // chan_count, lax.rem(other, chan_count)

    for k in range(1, LAYERS):
        greet(lax.rem(layer + k, LAYERS) * peers + spot, chan)
    for k in range(1, crew):
        p, c = crew_member(k)
        greet(layer * peers + p, c)

    us[:, tiles * width :, :] = jnp.zeros((groups, us.shape[1] - tiles * width, TILE), jnp.bfloat16)
    for which in (0, 1):
        span = slice((1 - which) * layer_rows, (2 - which) * layer_rows)

        @pl.when(layer == which)
        def _(span=span):
            us[:, span, :] = jnp.zeros((groups, layer_rows, TILE), jnp.bfloat16)

    loads[2].wait()
    scaled = raw_ref[...] * factor
    lanes = jnp.concatenate([scaled] * chan_count, axis=1)
    kept = lax.broadcasted_iota(jnp.int32, lanes.shape, 1) // share == chan
    lanes = jnp.where(kept, lanes, 0.0)
    for i in range(crew):
        filt_ref[i] = lanes[i * groups : (i + 1) * groups, :]
    loads[0].wait()
    loads[1].wait()
    u_loc[...] = (
        gate_ref[...].astype(jnp.float32) * up_ref[...].astype(jnp.float32)
    ).astype(jnp.bfloat16)
    pl.semaphore_wait(barrier, crew + LAYERS - 2)

    def place(ref, g, s):
        return ref.at[
            g,
            pl.ds(pl.multiple_of((s // per_tile) * width, width), width),
            pl.ds(pl.multiple_of(lax.rem(s, per_tile) * block, block), block),
        ]

    def strip(ref, q, g):
        return ref.at[pl.ds(pl.multiple_of(q * local_chan + g * width, width), width), :]

    def remote(from_ref, to_ref, send, recv, to_seq, to_chan=None):
        return pltpu.make_async_remote_copy(
            src_ref=from_ref,
            dst_ref=to_ref,
            send_sem=send,
            recv_sem=recv,
            device_id=(to_seq, chan if to_chan is None else to_chan),
            device_id_type=MESH,
        )

    def wait_bytes(ref, sem):
        pltpu.make_async_copy(ref, ref, sem).wait()

    def layer_span(ref, g, which):
        return ref.at[g, pl.ds(pl.multiple_of(which * layer_rows, layer_rows), layer_rows), :]

    def scatter(ref, buf, send, recv, g):
        for k in (2, 3, 1):
            p = lax.rem(spot + k, peers)
            remote(
                strip(ref, p, g), place(buf, g, seq), send.at[0], recv.at[g], layer * peers + p
            ).start()
        pltpu.make_async_copy(strip(ref, spot, g), place(buf, g, seq), recv.at[g]).start()

    def scatter_both(g):
        @pl.when(layer < LAYERS // 2)
        def _():
            scatter(x_hbm, xs, x_send, x_recv, g)
            scatter(u_loc, us, u_send, u_recv, g)

        @pl.when(layer >= LAYERS // 2)
        def _():
            scatter(u_loc, us, u_send, u_recv, g)
            scatter(x_hbm, xs, x_send, x_recv, g)

    def give_back(buf, ref, send, recv, g):
        for k in (2, 3, 1):
            p = lax.rem(spot + k, peers)
            remote(
                place(buf, g, p), strip(ref, spot, g), send.at[0], recv.at[0], layer * peers + p
            ).start()
        pltpu.make_async_copy(place(buf, g, spot), strip(ref, spot, g), recv.at[0]).start()

    def hop(g, origin, to_layer):
        buf = xs if origin < LAYERS // 2 else us
        ref = layer_span(buf, g, origin)
        return remote(ref, ref, z_send.at[0], z_recv.at[g, origin], to_layer * peers + spot)

    def hand(g, to_layer):
        return remote(
            part_out.at[g], part_in.at[g], p_send.at[0], p_recv.at[g], to_layer * peers + spot
        )

    scatter_both(0)
    for k in range(1, crew):
        p, c = crew_member(k)
        remote(
            filt_ref.at[c * peers + p], filt_in.at[slot], k_send.at[0], k_recv.at[0],
            layer * peers + p, c,
        ).start()
    pltpu.make_async_copy(filt_ref.at[chan * peers + spot], filt_in.at[slot], k_recv.at[0]).start()

    def scatter_rest(g, carry):
        scatter_both(g)
        return carry

    lax.fori_loop(1, groups, scatter_rest, 0)

    filt_targets = {0: (1, 2, 3), 1: (2,), 2: (1,), 3: (1, 2)}
    filt_sources = {0: (), 1: (0, 2, 3), 2: (0, 1, 3), 3: (0,)}

    def filt_hop(origin, to_layer):
        return remote(
            filt_all.at[origin], filt_all.at[origin], f_send.at[1], kz_recv.at[origin],
            to_layer * peers + spot,
        )

    def spread_filters():
        wait_bytes(filt_in, k_recv.at[0])
        for s in range(peers):
            part = filt_in[s * chan_count]
            for c in range(1, chan_count):
                part = part + filt_in[s * chan_count + c]
            filt_all[layer, s] = part
        for which in range(LAYERS):

            @pl.when(layer == which)
            def _(which=which):
                for to in filt_targets[which]:
                    filt_hop(which, to).start()

    def gather_layer(g):
        first_x = layer < LAYERS // 2

        @pl.when(first_x)
        def _():
            wait_bytes(layer_span(xs, g, layer), x_recv.at[g])

        @pl.when(jnp.logical_not(first_x))
        def _():
            wait_bytes(layer_span(us, g, layer), u_recv.at[g])

        @pl.when(layer == 0)
        def _():
            hop(g, 0, 2).start()
            hop(g, 0, 1).start()

        @pl.when(layer == 1)
        def _():
            hop(g, 1, 2).start()

        @pl.when(layer == 2)
        def _():
            hop(g, 2, 1).start()

        @pl.when(layer == 3)
        def _():
            hop(g, 3, 1).start()
            hop(g, 3, 2).start()

        @pl.when(g == 0)
        def _():
            spread_filters()

    row_id = lax.broadcasted_iota(jnp.int32, (TILE, TILE), 0)
    col_id = lax.broadcasted_iota(jnp.int32, (TILE, TILE), 1)
    flip = jnp.where(row_id + col_id == TILE - 1, 1.0, 0.0).astype(jnp.bfloat16)
    row_in = lax.broadcasted_iota(jnp.int32, (block, block), 0)
    col_in = lax.broadcasted_iota(jnp.int32, (block, block), 1)
    upper = col_in >= row_in
    lower_flipped = col_in + row_in >= block - 1

    def compute(g):
        for which in range(LAYERS):

            @pl.when(layer == which)
            def _(which=which):
                compute_for(which, g)

    def compute_for(which, g):
        low_end, high_end = which * half, (which + 1) * half - 1
        inner = which in (1, 2)
        x_first = 0 if which in (1, 2) else low_end
        u_last = tiles - 1 if which in (1, 2) else high_end
        conv_last = tiles - 1 if which == 2 else high_end
        grad_first = 0 if which == 1 else low_end

        @pl.when(g == 0)
        def _():
            for origin in filt_sources[which]:
                filt_hop(origin, which).wait_recv()

        if which < LAYERS // 2:
            wait_bytes(layer_span(us, g, which), u_recv.at[g])
        else:
            wait_bytes(layer_span(xs, g, which), x_recv.at[g])
        if inner:
            for origin in range(LAYERS):
                if origin != which:
                    hop(g, origin, which).wait_recv()

        def span(first, final):
            return slice(first * width, (final + 1) * width)

        lags = [
            lag
            for lag in range(tiles)
            if max(x_first, low_end - lag) <= min(high_end, conv_last - lag)
            or max(low_end, grad_first + lag) <= min(u_last, high_end + lag)
        ]
        before = jnp.zeros((block, block), jnp.float32)
        for m in range(per_tile * len(lags)):
            row = filt_all[m // peers, m % peers, pl.ds(g, 1), :]
            rolled = pltpu.roll(
                jnp.broadcast_to(row, (block, block)), 0, 1, stride=1, stride_axis=0
            )
            table[m] = jnp.where(upper, rolled, before).astype(jnp.bfloat16)
            before = rolled

        def gather_table(lag):
            rows = []
            for i in range(per_tile):
                parts = []
                for j in range(per_tile):
                    m = lag * per_tile + j - i
                    parts.append(table[m] if m >= 0 else jnp.zeros((block, block), jnp.bfloat16))
                rows.append(jnp.concatenate(parts, axis=1))
            return jnp.concatenate(rows, axis=0)

        def add(acc, seen, first, final, value):
            runs = []
            for tile in range(first, final + 1):
                if runs and runs[-1][2] == (tile in seen):
                    runs[-1][1] = tile
                else:
                    runs.append([tile, tile, tile in seen])
            for begin, end, known in runs:
                part = value[(begin - first) * width : (end - first + 1) * width]
                if known:
                    acc[span(begin, end), :] += part
                else:
                    acc[span(begin, end), :] = part
            seen.update(range(first, final + 1))

        seen_c, seen_g = set(), set()
        for lag in lags:
            filt = gather_table(lag)
            first, final = max(x_first, low_end - lag), min(high_end, conv_last - lag)
            u_from, u_to = max(low_end, grad_first + lag), min(u_last, high_end + lag)
            if first <= final:
                add(acc_c, seen_c, first + lag, final + lag, dot(xs[g, span(first, final), :], filt, NN))
            if u_from <= u_to:
                add(acc_g, seen_g, u_from - lag, u_to - lag, dot(us[g, span(u_from, u_to), :], filt, NT))

        mine = span(low_end, high_end)
        if which == 2:
            part_out[g] = acc_c[last * layer_rows :, :].astype(jnp.bfloat16)
            hand(g, 3).start()
        if which == 1:
            part_out[g] = acc_g[:layer_rows, :].astype(jnp.bfloat16)
            hand(g, 0).start()
        if which < last:
            cv[g] = acc_c[mine, :].astype(jnp.bfloat16)
            give_back(cv, conv_in, c_send, c_recv, g)
        else:
            held[g] = acc_c[mine, :]
        if which > 0:
            gv[g] = acc_g[mine, :].astype(jnp.bfloat16)
            give_back(gv, gi_ref, g_send, g_recv, g)
        else:
            held[g] = acc_g[mine, :]

        gram_first = 0 if inner else low_end
        turned = dot(flip, xs[g, span(gram_first, high_end), :], NT).astype(jnp.bfloat16)

        def window(first, count):
            return us[g, first * width : (first + count) * width, :]

        def gram_of(lag):
            if not inner:
                return dot(turned, window(low_end + lag, half), NN)
            if which == 1:
                return dot(turned, window(lag, 2 * half), NN)
            if lag < SPLIT_LAG:
                return dot(turned[:, 2 * half * width :], window(2 * half + lag, half), NN)
            return dot(turned[:, : 2 * half * width], window(lag, 2 * half), NN)

        gram_lags = half if not inner else (SPLIT_LAG if which == 1 else tiles)
        zero = jnp.zeros((block, block), jnp.float32)
        gram = gram_of(0)
        current = gram[block:, :block] + gram[:block, block:]
        for lag in range(gram_lags):
            following = gram_of(lag + 1) if lag + 1 < gram_lags else None
            odd = gram[block:, block:]
            if following is None:
                even = zero
            else:
                odd = odd + following[:block, :block]
                even = following[block:, :block] + following[:block, block:]
            for i, (a, b) in enumerate(((current, odd), (odd, even))):
                mixed = jnp.where(lower_flipped, a, b)
                aligned = pltpu.roll(mixed, 1, 1, stride=1, stride_axis=0)
                total = jnp.sum(aligned, axis=0, keepdims=True) * factor
                fg_out[lag * per_tile + i, pl.ds(g, 1), :] = total
            current, gram = even, following

        @pl.when(g == groups - 1)
        def _():
            for to in grad_targets[which]:
                grad_hop(which, to).start()

    grad_targets = {0: (), 1: (0,), 2: (0, 1, 3), 3: (0,)}
    grad_sources = {0: (1, 2, 3), 1: (2,), 2: (), 3: (2,)}

    def grad_hop(origin, to_layer):
        return remote(
            fg_out.at[pl.ds(to_layer * peers, peers)], fg_layer.at[origin], f_send.at[0],
            fz_recv.at[origin], to_layer * peers + spot,
        )

    def finish(g):
        @pl.when(layer == last)
        def _():
            hand(g, last).wait_recv()
            cv[g] = (held[g] + part_in[g].astype(jnp.float32)).astype(jnp.bfloat16)
            give_back(cv, conv_in, c_send, c_recv, g)

        @pl.when(layer == 0)
        def _():
            hand(g, 0).wait_recv()
            gv[g] = (held[g] + part_in[g].astype(jnp.float32)).astype(jnp.bfloat16)
            give_back(gv, gi_ref, g_send, g_recv, g)

    def stage(step, delay, body):
        @pl.when((step >= delay) & (step < groups + delay))
        def _():
            body(step - delay)

    def pipeline(step, carry):
        stage(step, 0, gather_layer)
        stage(step, DELAY_COMPUTE, compute)
        stage(step, DELAY_FINISH, finish)
        return carry

    lax.fori_loop(0, groups + DELAY_FINISH, pipeline, 0)

    for which in range(LAYERS):

        @pl.when(layer == which)
        def _(which=which):
            total = None
            if which != 3:
                total = fg_out[which * peers : (which + 1) * peers]
            for origin in grad_sources[which]:
                grad_hop(origin, which).wait_recv()
                part = fg_layer[origin]
                total = part if total is None else total + part
            fg_sum[...] = total

    for k in range(1, crew):
        p, c = crew_member(k)
        remote(
            fg_sum.at[p], fg_in.at[chan * peers + spot], f_send.at[2], f_recv.at[0],
            layer * peers + p, c,
        ).start()
    pltpu.make_async_copy(fg_sum.at[spot], fg_in.at[chan * peers + spot], f_recv.at[0]).start()

    wait_bytes(conv_in, c_recv.at[0])
    gg_ref[...] = (up_ref[...].astype(jnp.float32) * conv_in[...].astype(jnp.float32)).astype(
        jnp.bfloat16
    )
    wait_bytes(gi_ref, g_recv.at[0])
    wait_bytes(fg_in, f_recv.at[0])
    for i in range(crew):
        total = fg_in[i]
        kept_part = total[:, :share]
        for d in range(1, chan_count):
            kept_part = jnp.where(chan == d, total[:, d * share : (d + 1) * share], kept_part)
        grad_ref[i * groups : (i + 1) * groups, :] = kept_part

    sent = pl.ds(0, groups * (peers - 1) // peers)
    wait_bytes(cv.at[sent], x_send.at[0])
    wait_bytes(cv.at[sent], u_send.at[0])
    wait_bytes(cv.at[sent], c_send.at[0])
    wait_bytes(cv.at[sent], g_send.at[0])
    wait_bytes(filt_in.at[pl.ds(0, crew - 1)], k_send.at[0])
    wait_bytes(filt_in.at[pl.ds(0, crew - 1)], f_send.at[2])
    for which in range(LAYERS):

        @pl.when(layer == which)
        def _(which=which):
            hops = 1 if which in (1, 2) else 2
            for _ in range(hops):
                wait_bytes(cv, z_send.at[0])
            if which in (1, 2):
                wait_bytes(cv, p_send.at[0])
            for _ in filt_targets[which]:
                wait_bytes(filt_all.at[0], f_send.at[1])
            for _ in grad_targets[which]:
                wait_bytes(fg_layer.at[0], f_send.at[0])


def store_kernel(a_ref, b_ref, c_ref, a_out, b_out, c_out, sems):
    copies = [
        pltpu.make_async_copy(a_ref, a_out, sems.at[0]),
        pltpu.make_async_copy(b_ref, b_out, sems.at[1]),
        pltpu.make_async_copy(c_ref, c_out, sems.at[2]),
    ]
    for copy in copies:
        copy.start()
    for copy in copies:
        copy.wait()


def layered_shards(inputs, gating, grad_out, filters):
    seq_count = lax.axis_size("seq")
    chan_count = lax.axis_size("chan")
    chan_rows, block = inputs.shape
    peers = seq_count // LAYERS
    crew = peers * chan_count
    groups = chan_rows // peers // GROUP_WIDTH
    length = block * seq_count
    tiles = length // TILE
    rows = tiles * GROUP_WIDTH
    layer_rows = rows // LAYERS
    blocks = length // block
    vmem = pl.BlockSpec(memory_space=pltpu.VMEM)
    hbm = pl.BlockSpec(memory_space=pltpu.HBM)
    single = pltpu.SemaphoreType.DMA((1,))
    by_group = pltpu.SemaphoreType.DMA((groups,))
    by_layer = pltpu.SemaphoreType.DMA((LAYERS,))
    flat = pltpu.VMEM((chan_rows, block), jnp.bfloat16)
    layered = pltpu.VMEM((groups, layer_rows, TILE), jnp.bfloat16)
    small = pltpu.VMEM((crew, groups, block), jnp.float32)
    outs = (
        jax.ShapeDtypeStruct((chan_rows, block), jnp.bfloat16),
        jax.ShapeDtypeStruct((chan_rows, block), jnp.bfloat16),
        jax.ShapeDtypeStruct(filters.shape, jnp.float32),
    )
    results = pl.pallas_call(
        functools.partial(layered_kernel, seq_count, chan_count),
        out_shape=outs,
        in_specs=[hbm] * 4,
        out_specs=(vmem, vmem, vmem),
        scratch_shapes=[
            flat,
            flat,
            pltpu.VMEM(filters.shape, jnp.float32),
            small,
            small,
            pltpu.VMEM((LAYERS, peers, groups, block), jnp.float32),
            flat,
            pltpu.VMEM((groups, rows, TILE), jnp.bfloat16),
            pltpu.VMEM((groups, rows + 2 * layer_rows, TILE), jnp.bfloat16),
            pltpu.VMEM((blocks, block, block), jnp.bfloat16),
            pltpu.VMEM((rows, TILE), jnp.float32),
            pltpu.VMEM((rows, TILE), jnp.float32),
            layered,
            layered,
            flat,
            pltpu.VMEM((groups, layer_rows, TILE), jnp.float32),
            layered,
            layered,
            pltpu.VMEM((blocks, groups, block), jnp.float32),
            pltpu.VMEM((LAYERS, peers, groups, block), jnp.float32),
            pltpu.VMEM((peers, groups, block), jnp.float32),
            small,
            pltpu.SemaphoreType.DMA((3,)),
            single,
            single,
            single,
            single,
            single,
            single,
            pltpu.SemaphoreType.DMA((3,)),
            single,
            by_group,
            by_group,
            single,
            single,
            pltpu.SemaphoreType.DMA((groups, LAYERS)),
            by_group,
            single,
            by_layer,
            single,
            by_layer,
        ],
        compiler_params=pltpu.CompilerParams(
            collective_id=0, has_side_effects=True, vmem_limit_bytes=VMEM_LIMIT
        ),
    )(inputs, gating, grad_out, filters)
    return pl.pallas_call(
        store_kernel,
        out_shape=outs,
        in_specs=[vmem] * 3,
        out_specs=(hbm, hbm, hbm),
        scratch_shapes=[pltpu.SemaphoreType.DMA((3,))],
    )(*results)


VMEM_LIMIT = 56 * 1024 * 1024


def solution(mesh):
    placed = (P("chan", "seq"), P("chan", "seq"), P("chan", "seq"), P(None, ("seq", "chan")))
    layered = mesh.shape["seq"] == 16 and mesh.shape["chan"] == 2
    return jax.shard_map(
        layered_shards if layered else shards,
        mesh=mesh,
        in_specs=placed,
        out_specs=(P("chan", "seq"), P("chan", "seq"), P(None, ("seq", "chan"))),
        check_vma=False,
    )
```

```python
import functools
import math

import jax
import jax.numpy as jnp
from jax import lax
from jax.experimental import pallas as pl
from jax.experimental.pallas import tpu as pltpu
from jax.sharding import PartitionSpec as P

D = 4096
G = 64


HIGHEST = lax.Precision.HIGHEST


def make_tables(seq_count, block_len):
    outer = 2 * seq_count
    total = outer * block_len
    outer_index = jnp.arange(outer, dtype=jnp.int32)
    block_index = jnp.arange(seq_count, dtype=jnp.int32)
    inner_index = jnp.arange(block_len, dtype=jnp.int32)
    block_angle = (outer_index[:, None] * block_index[None, :] % outer).astype(jnp.float32) * (
        2.0 * math.pi / outer
    )
    twist_angle = (outer_index[:, None] * inner_index[None, :] % total).astype(jnp.float32) * (
        2.0 * math.pi / total
    )
    inner_angle = (inner_index[:, None] * inner_index[None, :] % block_len).astype(jnp.float32) * (
        2.0 * math.pi / block_len
    )
    return (
        jnp.cos(block_angle),
        jnp.sin(block_angle),
        jnp.cos(twist_angle),
        jnp.sin(twist_angle),
        jnp.cos(inner_angle),
        jnp.sin(inner_angle),
    )


def right_product(values, table):
    return jnp.einsum("ckm,mj->ckj", values, table, precision=HIGHEST)


def forward_dft(signal, tables):
    block_cos, block_sin, twist_cos, twist_sin, inner_cos, inner_sin = tables
    real_first = jnp.einsum("kn,cnm->ckm", block_cos, signal, precision=HIGHEST)
    imag_first = -jnp.einsum("kn,cnm->ckm", block_sin, signal, precision=HIGHEST)
    real_twist = real_first * twist_cos + imag_first * twist_sin
    imag_twist = imag_first * twist_cos - real_first * twist_sin
    real_spec = right_product(real_twist, inner_cos) + right_product(imag_twist, inner_sin)
    imag_spec = right_product(imag_twist, inner_cos) - right_product(real_twist, inner_sin)
    return (real_spec, imag_spec)


def inverse_dft(real_spec, imag_spec, tables):
    block_cos, block_sin, twist_cos, twist_sin, inner_cos, inner_sin = tables
    real_first = right_product(real_spec, inner_cos) - right_product(imag_spec, inner_sin)
    imag_first = right_product(real_spec, inner_sin) + right_product(imag_spec, inner_cos)
    real_twist = real_first * twist_cos - imag_first * twist_sin
    imag_twist = real_first * twist_sin + imag_first * twist_cos
    total = real_spec.shape[1] * real_spec.shape[2]
    result = jnp.einsum("kn,ckm->cnm", block_cos, real_twist, precision=HIGHEST)
    result = result - jnp.einsum("kn,ckm->cnm", block_sin, imag_twist, precision=HIGHEST)
    return result / total


def shards(inputs, gating, grad_out, filters):
    seq_count = lax.axis_size("seq")
    chan_count = lax.axis_size("chan")
    chan_rows, block_len = inputs.shape
    local_chan = chan_rows // seq_count
    group_width = D // G
    groups_here = G // chan_count
    local_groups = max(1, local_chan // group_width)
    group_share = local_chan // local_groups
    copies = max(1, seq_count // groups_here)
    length = block_len * seq_count
    outer = 2 * seq_count
    factor = 1.0 / math.sqrt(group_width * length)
    tables = make_tables(seq_count, block_len)
    whole = lax.all_gather(filters, ("seq", "chan"), axis=1, tiled=True)
    first_group = (
        lax.axis_index("chan") * chan_rows + lax.axis_index("seq") * local_chan
    ) // group_width
    kernel_rows = lax.dynamic_slice_in_dim(whole, first_group, local_groups, 0)
    kernel_blocks = kernel_rows.reshape(local_groups, seq_count, block_len)
    kernel_real, kernel_imag = forward_dft(kernel_blocks * factor, tables)
    kernel_real = kernel_real[:, None]
    kernel_imag = kernel_imag[:, None]
    shaped_inputs = inputs.reshape(chan_rows, 1, block_len)
    values, gate_part, upstream = (
        lax.all_to_all(shaped_inputs, "seq", split_axis=0, concat_axis=1, tiled=True),
        lax.all_to_all(
            gating.reshape(chan_rows, 1, block_len), "seq", split_axis=0, concat_axis=1, tiled=True
        ),
        lax.all_to_all(
            grad_out.reshape(chan_rows, 1, block_len),
            "seq",
            split_axis=0,
            concat_axis=1,
            tiled=True,
        ),
    )
    input_real, input_imag = forward_dft(values.astype(jnp.float32), tables)
    upstream_f = upstream.astype(jnp.float32)
    product_b = lax.optimization_barrier(
        (gate_part.astype(jnp.float32) * upstream_f).astype(jnp.bfloat16)
    )
    up_real, up_imag = forward_dft(product_b.astype(jnp.float32), tables)
    grouped_shape = (local_groups, group_share, outer, block_len)
    input_real = input_real.reshape(grouped_shape)
    input_imag = input_imag.reshape(grouped_shape)
    up_real = up_real.reshape(grouped_shape)
    up_imag = up_imag.reshape(grouped_shape)
    flat_shape = (local_chan, outer, block_len)
    conv_real = input_real * kernel_real - input_imag * kernel_imag
    conv_imag = input_real * kernel_imag + input_imag * kernel_real
    convolved = inverse_dft(conv_real.reshape(flat_shape), conv_imag.reshape(flat_shape), tables)
    conv_b = convolved.astype(jnp.bfloat16)
    second = (upstream_f * lax.optimization_barrier(conv_b).astype(jnp.float32)).astype(
        jnp.bfloat16
    )
    back_real = up_real * kernel_real + up_imag * kernel_imag
    back_imag = up_imag * kernel_real - up_real * kernel_imag
    grad_input = inverse_dft(
        back_real.reshape(flat_shape), back_imag.reshape(flat_shape), tables
    ).astype(jnp.bfloat16)
    returned_input, returned_second = (
        lax.all_to_all(grad_input, "seq", split_axis=1, concat_axis=0, tiled=True),
        lax.all_to_all(second, "seq", split_axis=1, concat_axis=0, tiled=True),
    )
    returned_second = returned_second.reshape(chan_rows, block_len)
    cross_real = jnp.sum(input_real * up_real + input_imag * up_imag, axis=1)
    cross_imag = jnp.sum(input_real * up_imag - input_imag * up_real, axis=1)
    partial_grad = inverse_dft(cross_real, cross_imag, tables) * factor
    received = lax.all_to_all(partial_grad, "seq", split_axis=1, concat_axis=0, tiled=True)
    summed = received.reshape(groups_here, copies, block_len).sum(axis=1)
    grad_filters = lax.all_to_all(summed, "chan", split_axis=1, concat_axis=0, tiled=True)
    return (returned_input.reshape(chan_rows, block_len), returned_second, grad_filters)


GROUP_WIDTH = D // G
MESH = pl.DeviceIdType.MESH
TILE = 256
LAYERS = 4
LEAD, DELAY_RELAY, DELAY_COMPUTE = 4, 2, 3
NT = (((1,), (1,)), ((), ()))
NN = (((1,), (0,)), ((), ()))


def dot(a, b, dims):
    return lax.dot_general(a, b, dims, preferred_element_type=jnp.float32)


def layered_kernel(
    seq_count,
    chan_count,
    x_hbm,
    gate_hbm,
    up_hbm,
    raw_hbm,
    gi_ref,
    gg_ref,
    grad_ref,
    gate_ref,
    up_ref,
    raw_ref,
    filt_ref,
    filt_in,
    filt_layer,
    filt_all,
    u_loc,
    xs,
    us,
    table,
    acc_c,
    acc_g,
    cv,
    gv,
    conv_in,
    far,
    fg_out,
    fg_layer,
    fg_sum,
    fg_in,
    load_sem,
    x_send,
    u_send,
    c_send,
    g_send,
    z_send,
    far_send,
    f_send,
    k_send,
    x_recv,
    u_recv,
    c_recv,
    g_recv,
    zx_recv,
    zu_recv,
    f_recv,
    fz_recv,
    k_recv,
    kz_recv,
    enter_sem,
):
    seq = lax.axis_index("seq")
    chan = lax.axis_index("chan")
    peers = seq_count // LAYERS
    crew = peers * chan_count
    layer = seq // peers
    spot = lax.rem(seq, peers)
    slot = spot * chan_count + chan
    last = LAYERS - 1
    groups = xs.shape[0]
    block = x_hbm.shape[1]
    per_tile = TILE // block
    length = block * seq_count
    tiles = length // TILE
    half = tiles // LAYERS
    width = GROUP_WIDTH
    layer_rows = half * width
    local_chan = groups * width
    share = raw_hbm.shape[1]
    factor = 1.0 / math.sqrt(width * length)

    loads = [
        pltpu.make_async_copy(gate_hbm, gate_ref, load_sem.at[0]),
        pltpu.make_async_copy(up_hbm, up_ref, load_sem.at[1]),
        pltpu.make_async_copy(raw_hbm, raw_ref, load_sem.at[2]),
    ]
    for load in loads:
        load.start()

    barrier = pltpu.get_barrier_semaphore()

    def greet(to_seq, to_chan):
        pl.semaphore_signal(barrier, inc=1, device_id=(to_seq, to_chan), device_id_type=MESH)

    def crew_member(k):
        other = lax.rem(slot + k, crew)
        return other // chan_count, lax.rem(other, chan_count)

    for k in range(1, crew):
        p, c = crew_member(k)
        greet(layer * peers + p, c)
    everyone, lone = range(peers), (spot,)
    greeted = {
        0: ((1, everyone), (2, lone)),
        1: ((0, lone), (2, lone), (3, lone)),
        2: ((0, lone), (1, lone), (3, everyone)),
        3: (),
    }
    for which in range(LAYERS):

        @pl.when(layer == which)
        def _(which=which):
            for to_layer, spots in greeted[which]:
                for p in spots:
                    greet(to_layer * peers + p, chan)

    loads[2].wait()
    scaled = raw_ref[...] * factor
    lanes = jnp.concatenate([scaled] * chan_count, axis=1)
    kept = lax.broadcasted_iota(jnp.int32, lanes.shape, 1) // share == chan
    lanes = jnp.where(kept, lanes, 0.0)
    for i in range(crew):
        filt_ref[i] = lanes[i * groups : (i + 1) * groups, :]
    loads[0].wait()
    loads[1].wait()
    u_loc[...] = (
        gate_ref[...].astype(jnp.float32) * up_ref[...].astype(jnp.float32)
    ).astype(jnp.bfloat16)
    expected = {0: 2, 1: peers + 1, 2: 2, 3: 1 + peers}
    for which in range(LAYERS):

        @pl.when(layer == which)
        def _(which=which):
            pl.semaphore_wait(barrier, crew - 1 + expected[which])

    def enter(origin, to_layer, p):
        pl.semaphore_signal(
            enter_sem.at[origin],
            inc=1,
            device_id=(to_layer * peers + p, chan),
            device_id_type=MESH,
        )

    @pl.when(layer == 3)
    def _():
        for p in everyone:
            enter(3, 2, p)

    def place(ref, g, s):
        return ref.at[
            g,
            pl.ds(pl.multiple_of((s // per_tile) * width, width), width),
            pl.ds(pl.multiple_of(lax.rem(s, per_tile) * block, block), block),
        ]

    def strip(ref, q, g):
        return ref.at[pl.ds(pl.multiple_of(q * local_chan + g * width, width), width), :]

    def remote(from_ref, to_ref, send, recv, to_seq, to_chan=None):
        return pltpu.make_async_remote_copy(
            src_ref=from_ref,
            dst_ref=to_ref,
            send_sem=send,
            recv_sem=recv,
            device_id=(to_seq, chan if to_chan is None else to_chan),
            device_id_type=MESH,
        )

    def wait_bytes(ref, sem):
        pltpu.make_async_copy(ref, ref, sem).wait()

    def layer_span(ref, g, which):
        return ref.at[g, pl.ds(pl.multiple_of(which * layer_rows, layer_rows), layer_rows), :]

    def scatter(ref, buf, send, recv, g):
        for k in (2, 3, 1):
            p = lax.rem(spot + k, peers)
            remote(
                strip(ref, p, g), place(buf, g, seq), send.at[0], recv.at[g], layer * peers + p
            ).start()
        pltpu.make_async_copy(strip(ref, spot, g), place(buf, g, seq), recv.at[g]).start()

    def scatter_both(g):
        @pl.when(layer < LAYERS // 2)
        def _():
            scatter(x_hbm, xs, x_send, x_recv, g)
            scatter(u_loc, us, u_send, u_recv, g)

        @pl.when(layer >= LAYERS // 2)
        def _():
            scatter(u_loc, us, u_send, u_recv, g)
            scatter(x_hbm, xs, x_send, x_recv, g)

    def give_back(buf, ref, send, recv, g):
        for k in (2, 3, 1):
            p = lax.rem(spot + k, peers)
            remote(
                place(buf, g, p), strip(ref, spot, g), send.at[0], recv.at[0], layer * peers + p
            ).start()
        pltpu.make_async_copy(place(buf, g, spot), strip(ref, spot, g), recv.at[0]).start()

    def send_far(g, ref, recv, to_layer):
        for k in (2, 3, 1, 0):
            p = lax.rem(spot + k, peers)
            remote(
                place(far, g, p), strip(ref, spot, g), far_send.at[0], recv.at[0],
                to_layer * peers + p,
            ).start()

    def hop_x(g, origin, to_layer):
        ref = layer_span(xs, g, origin)
        return remote(ref, ref, z_send.at[0], zx_recv.at[g, origin], to_layer * peers + spot)

    def hop_u(g, origin, to_layer):
        ref = layer_span(us, g, origin)
        return remote(ref, ref, z_send.at[0], zu_recv.at[g, origin], to_layer * peers + spot)

    def ahead(from_ref, buf, recv, origin, to_layer):
        def step(g, carry):
            remote(
                strip(from_ref, spot, g), place(buf, g, seq), z_send.at[0], recv.at[g, origin],
                to_layer * peers + spot,
            ).start()
            return carry

        lax.fori_loop(0, groups, step, 0)

    def rest(g, buf, recv, origin, to_layer):
        sibling = spot + 1 - 2 * lax.rem(spot, per_tile)
        tile = origin * half + 1 - spot // per_tile
        refs = (
            place(buf, g, origin * peers + sibling),
            buf.at[g, pl.ds(pl.multiple_of(tile * width, width), width), :],
        )
        for ref in refs:
            remote(
                ref, ref, z_send.at[0], recv.at[g, origin], to_layer * peers + spot
            ).start()

    scatter_both(0)

    @pl.when(layer == 0)
    def _():
        ahead(x_hbm, xs, zx_recv, 0, 1)

    @pl.when(layer == 1)
    def _():
        ahead(x_hbm, xs, zx_recv, 1, 2)

    @pl.when(layer == 2)
    def _():
        ahead(u_loc, us, zu_recv, 2, 1)

    @pl.when(layer == 3)
    def _():
        ahead(u_loc, us, zu_recv, 3, 2)

    for k in range(1, crew):
        p, c = crew_member(k)
        remote(
            filt_ref.at[c * peers + p], filt_in.at[slot], k_send.at[0], k_recv.at[0],
            layer * peers + p, c,
        ).start()
    pltpu.make_async_copy(filt_ref.at[chan * peers + spot], filt_in.at[slot], k_recv.at[0]).start()

    def scatter_early(g, carry):
        scatter_both(g)
        return carry

    lax.fori_loop(1, LEAD, scatter_early, 0)

    filt_targets = {0: (1, 2), 1: (2,), 2: (1,), 3: (1, 2)}
    filt_sources = {0: (), 1: (0, 2, 3), 2: (0, 1, 3), 3: (0,)}

    def filt_hop(origin, to_layer):
        return remote(
            filt_layer.at[origin], filt_layer.at[origin], f_send.at[1], kz_recv.at[origin],
            to_layer * peers + spot,
        )

    def spread_filters():
        wait_bytes(filt_in, k_recv.at[0])
        parts = []
        for s in range(peers):
            part = filt_in[s * chan_count]
            for c in range(1, chan_count):
                part = part + filt_in[s * chan_count + c]
            parts.append(part)
        for s in range(peers // 2):
            pair = jnp.concatenate(parts[2 * s : 2 * s + 2], axis=0)
            filt_layer[layer, s] = pair.astype(jnp.bfloat16)
        for which in range(LAYERS):

            @pl.when(layer == which)
            def _(which=which):
                for to in filt_targets[which]:
                    filt_hop(which, to).start()

    def wait_x(g):
        wait_bytes(layer_span(xs, g, layer), x_recv.at[g])

    def wait_u(g):
        wait_bytes(layer_span(us, g, layer), u_recv.at[g])

    def gather_layer(g):
        @pl.when(layer == 0)
        def _():
            wait_x(g)
            rest(g, xs, zx_recv, 0, 1)
            wait_u(g)
            hop_u(g, 0, 1).start()

        @pl.when(layer == 1)
        def _():
            wait_x(g)
            rest(g, xs, zx_recv, 1, 2)

        @pl.when(layer == 2)
        def _():
            wait_u(g)
            rest(g, us, zu_recv, 2, 1)

        @pl.when(layer == 3)
        def _():
            wait_u(g)
            rest(g, us, zu_recv, 3, 2)
            wait_x(g)
            hop_x(g, 3, 2).start()

        @pl.when(g == 0)
        def _():
            spread_filters()

    def relay(g):
        @pl.when(layer == 1)
        def _():
            hop_x(g, 0, 1).wait_recv()
            hop_x(g, 0, 2).start()

        @pl.when(layer == 2)
        def _():
            hop_u(g, 3, 2).wait_recv()
            hop_u(g, 3, 1).start()

    row_id = lax.broadcasted_iota(jnp.int32, (TILE, TILE), 0)
    col_id = lax.broadcasted_iota(jnp.int32, (TILE, TILE), 1)
    flip = jnp.where(row_id + col_id == TILE - 1, 1.0, 0.0).astype(jnp.bfloat16)
    row_in = lax.broadcasted_iota(jnp.int32, (block, block), 0)
    col_in = lax.broadcasted_iota(jnp.int32, (block, block), 1)
    upper = col_in >= row_in
    lower_flipped = col_in + row_in >= block - 1

    def compute(g):
        for which in range(LAYERS):

            @pl.when(layer == which)
            def _(which=which):
                compute_for(which, g)

    def span(first, final):
        return slice(first * width, (final + 1) * width)

    def make_table(g, lags):
        before = jnp.zeros((block, block), jnp.float32)
        for m in range(per_tile * lags):
            row = filt_all[m // peers, m % peers, pl.ds(g, 1), :]
            rolled = pltpu.roll(
                jnp.broadcast_to(row, (block, block)), 0, 1, stride=1, stride_axis=0
            )
            table[m] = jnp.where(upper, rolled, before).astype(jnp.bfloat16)
            before = rolled

    def filter_of(lag):
        rows = []
        for i in range(per_tile):
            parts = []
            for j in range(per_tile):
                m = lag * per_tile + j - i
                parts.append(table[m] if m >= 0 else jnp.zeros((block, block), jnp.bfloat16))
            rows.append(jnp.concatenate(parts, axis=1))
        return jnp.concatenate(rows, axis=0)

    def add(acc, seen, first, final, value):
        runs = []
        for tile in range(first, final + 1):
            if runs and runs[-1][2] == (tile in seen):
                runs[-1][1] = tile
            else:
                runs.append([tile, tile, tile in seen])
        for begin, end, known in runs:
            part = value[(begin - first) * width : (end - first + 1) * width]
            if known:
                acc[span(begin, end), :] += part
            else:
                acc[span(begin, end), :] = part
        seen.update(range(first, final + 1))

    def convolve(g, x_tiles, out_tiles):
        seen = set()
        for lag in range(out_tiles[1] - x_tiles[0] + 1):
            first = max(x_tiles[0], out_tiles[0] - lag)
            final = min(x_tiles[1], out_tiles[1] - lag)
            if first <= final:
                add(
                    acc_c, seen, first + lag, final + lag,
                    dot(xs[g, span(first, final), :], filter_of(lag), NN),
                )

    def correlate(g, u_tiles, out_tiles):
        seen = set()
        for lag in range(u_tiles[1] - out_tiles[0] + 1):
            first = max(u_tiles[0], out_tiles[0] + lag)
            final = min(u_tiles[1], out_tiles[1] + lag)
            if first <= final:
                add(
                    acc_g, seen, first - lag, final - lag,
                    dot(us[g, span(first, final), :], filter_of(lag), NT),
                )

    def filter_grad(g, x_tiles, u_tiles):
        turned = {}

        def turned_from(tile):
            if tile not in turned:
                rows = xs[g, span(tile, x_tiles[1]), :]
                turned[tile] = dot(flip, rows, NT).astype(jnp.bfloat16)
            return turned[tile]

        def gram_of(lag):
            first = max(x_tiles[0], u_tiles[0] - lag)
            final = min(x_tiles[1], u_tiles[1] - lag)
            base = x_tiles[0] + (first - x_tiles[0]) % per_tile
            left = turned_from(base)[:, (first - base) * width : (final + 1 - base) * width]
            return dot(left, us[g, span(first + lag, final + lag), :], NN)

        lags = u_tiles[1] - x_tiles[0] + 1
        zero = jnp.zeros((block, block), jnp.float32)
        gram = gram_of(0)
        current = gram[block:, :block] + gram[:block, block:]
        for lag in range(lags):
            following = gram_of(lag + 1) if lag + 1 < lags else None
            odd = gram[block:, block:]
            if following is None:
                even = zero
            else:
                odd = odd + following[:block, :block]
                even = following[block:, :block] + following[:block, block:]
            for i, (a, b) in enumerate(((current, odd), (odd, even))):
                mixed = jnp.where(lower_flipped, a, b)
                aligned = pltpu.roll(mixed, 1, 1, stride=1, stride_axis=0)
                total = jnp.sum(aligned, axis=0, keepdims=True) * factor
                fg_out[lag * per_tile + i, pl.ds(g, 1), :] = total
            current, gram = even, following

    def send_grads(g, which):
        @pl.when(g == groups - 1)
        def _():
            for to in grad_targets[which]:
                grad_hop(which, to).start()

    def back_conv(g, tile):
        cv[g] = acc_c[span(tile, tile + half - 1), :].astype(jnp.bfloat16)
        give_back(cv, conv_in, c_send, c_recv, g)

    def back_grad(g, tile):
        gv[g] = acc_g[span(tile, tile + half - 1), :].astype(jnp.bfloat16)
        give_back(gv, gi_ref, g_send, g_recv, g)

    def compute_for(which, g):
        low, high = which * half, (which + 1) * half - 1

        @pl.when(g == 0)
        def _():
            for origin in filt_sources[which]:
                filt_hop(origin, which).wait_recv()
            if which == 2:
                pl.semaphore_wait(enter_sem.at[3], peers)
                filt_hop(0, 3).start()
            for origin in sorted(filt_sources[which] + ((which,) if which < last else ())):
                filt_all[origin] = (
                    filt_layer[origin].astype(jnp.float32).reshape(peers, groups, block)
                )

        make_table(g, half if which in (0, last) else tiles)
        if which == 0:
            convolve(g, (low, high), (low, high))
            back_conv(g, low)
        if which == 1:
            wait_u(g)
            hop_u(g, 0, 1).wait_recv()
            convolve(g, (0, high), (low, high))
            back_conv(g, low)
            filter_grad(g, (0, high), (0, high))
            send_grads(g, which)
            hop_u(g, 2, 1).wait_recv()
            hop_u(g, 3, 1).wait_recv()
            correlate(g, (0, tiles - 1), (0, high))
            far[g] = acc_g[span(0, low - 1), :].astype(jnp.bfloat16)
            send_far(g, gi_ref, g_recv, 0)
            back_grad(g, low)
        if which == 2:
            wait_x(g)
            hop_x(g, 3, 2).wait_recv()
            correlate(g, (low, tiles - 1), (low, high))
            back_grad(g, low)
            hop_x(g, 1, 2).wait_recv()
            hop_x(g, 0, 2).wait_recv()
            filter_grad(g, (0, tiles - 1), (low, tiles - 1))
            send_grads(g, which)
            convolve(g, (0, tiles - 1), (low, tiles - 1))
            far[g] = acc_c[span(high + 1, tiles - 1), :].astype(jnp.bfloat16)
            send_far(g, conv_in, c_recv, 3)
            back_conv(g, low)
        if which == 3:
            correlate(g, (low, high), (low, high))
            back_grad(g, low)

    grad_targets = {0: (), 1: (0,), 2: (0, 1, 3), 3: ()}
    grad_sources = {0: (1, 2), 1: (2,), 2: (), 3: (2,)}

    def grad_hop(origin, to_layer):
        return remote(
            fg_out.at[pl.ds(to_layer * peers, peers)], fg_layer.at[origin], f_send.at[0],
            fz_recv.at[origin], to_layer * peers + spot,
        )

    def stage(step, delay, body):
        @pl.when((step >= delay) & (step < groups + delay))
        def _():
            body(step - delay)

    def scatter_later(g):
        @pl.when(g >= LEAD)
        def _():
            scatter_both(g)

    def pipeline(step, carry):
        stage(step, 0, gather_layer)
        stage(step, -LEAD, scatter_later)
        stage(step, DELAY_RELAY, relay)
        stage(step, DELAY_COMPUTE, compute)
        return carry

    lax.fori_loop(0, groups + DELAY_COMPUTE, pipeline, 0)

    for which in range(LAYERS):

        @pl.when(layer == which)
        def _(which=which):
            total = None
            if which in (1, 2):
                total = fg_out[which * peers : (which + 1) * peers]
            for origin in grad_sources[which]:
                grad_hop(origin, which).wait_recv()
                part = fg_layer[origin]
                total = part if total is None else total + part
            fg_sum[...] = total

    for k in range(1, crew):
        p, c = crew_member(k)
        remote(
            fg_sum.at[p], fg_in.at[chan * peers + spot], f_send.at[2], f_recv.at[0],
            layer * peers + p, c,
        ).start()
    pltpu.make_async_copy(fg_sum.at[spot], fg_in.at[chan * peers + spot], f_recv.at[0]).start()

    wait_bytes(conv_in, c_recv.at[0])
    gg_ref[...] = (up_ref[...].astype(jnp.float32) * conv_in[...].astype(jnp.float32)).astype(
        jnp.bfloat16
    )
    wait_bytes(gi_ref, g_recv.at[0])
    wait_bytes(fg_in, f_recv.at[0])
    for i in range(crew):
        total = fg_in[i]
        kept_part = total[:, :share]
        for d in range(1, chan_count):
            kept_part = jnp.where(chan == d, total[:, d * share : (d + 1) * share], kept_part)
        grad_ref[i * groups : (i + 1) * groups, :] = kept_part

    sent = pl.ds(0, groups * (peers - 1) // peers)
    wait_bytes(cv.at[sent], x_send.at[0])
    wait_bytes(cv.at[sent], u_send.at[0])
    wait_bytes(filt_in.at[pl.ds(0, crew - 1)], k_send.at[0])
    wait_bytes(filt_in.at[pl.ds(0, crew - 1)], f_send.at[2])
    wait_bytes(cv, z_send.at[0])
    wait_bytes(cv, z_send.at[0])
    for which in range(LAYERS):

        @pl.when(layer == which)
        def _(which=which):
            if which < last:
                wait_bytes(cv.at[sent], c_send.at[0])
            if which > 0:
                wait_bytes(cv.at[sent], g_send.at[0])
            if which in (1, 2):
                wait_bytes(cv, far_send.at[0])
            for _ in filt_targets[which] + ((3,) if which == 2 else ()):
                wait_bytes(filt_layer.at[0], f_send.at[1])
            for _ in grad_targets[which]:
                wait_bytes(fg_layer.at[0], f_send.at[0])


def store_kernel(a_ref, b_ref, c_ref, a_out, b_out, c_out, sems):
    copies = [
        pltpu.make_async_copy(a_ref, a_out, sems.at[0]),
        pltpu.make_async_copy(b_ref, b_out, sems.at[1]),
        pltpu.make_async_copy(c_ref, c_out, sems.at[2]),
    ]
    for copy in copies:
        copy.start()
    for copy in copies:
        copy.wait()


def layered_shards(inputs, gating, grad_out, filters):
    seq_count = lax.axis_size("seq")
    chan_count = lax.axis_size("chan")
    chan_rows, block = inputs.shape
    peers = seq_count // LAYERS
    crew = peers * chan_count
    groups = chan_rows // peers // GROUP_WIDTH
    length = block * seq_count
    tiles = length // TILE
    rows = tiles * GROUP_WIDTH
    layer_rows = rows // LAYERS
    blocks = length // block
    vmem = pl.BlockSpec(memory_space=pltpu.VMEM)
    hbm = pl.BlockSpec(memory_space=pltpu.HBM)
    single = pltpu.SemaphoreType.DMA((1,))
    by_group = pltpu.SemaphoreType.DMA((groups,))
    by_layer = pltpu.SemaphoreType.DMA((LAYERS,))
    flat = pltpu.VMEM((chan_rows, block), jnp.bfloat16)
    layered = pltpu.VMEM((groups, layer_rows, TILE), jnp.bfloat16)
    small = pltpu.VMEM((crew, groups, block), jnp.float32)
    outs = (
        jax.ShapeDtypeStruct((chan_rows, block), jnp.bfloat16),
        jax.ShapeDtypeStruct((chan_rows, block), jnp.bfloat16),
        jax.ShapeDtypeStruct(filters.shape, jnp.float32),
    )
    results = pl.pallas_call(
        functools.partial(layered_kernel, seq_count, chan_count),
        out_shape=outs,
        in_specs=[hbm] * 4,
        out_specs=(vmem, vmem, vmem),
        scratch_shapes=[
            flat,
            flat,
            pltpu.VMEM(filters.shape, jnp.float32),
            small,
            small,
            pltpu.VMEM((LAYERS, peers // 2, 2 * groups, block), jnp.bfloat16),
            pltpu.VMEM((LAYERS, peers, groups, block), jnp.float32),
            flat,
            pltpu.VMEM((groups, rows, TILE), jnp.bfloat16),
            pltpu.VMEM((groups, rows, TILE), jnp.bfloat16),
            pltpu.VMEM((blocks, block, block), jnp.bfloat16),
            pltpu.VMEM((rows, TILE), jnp.float32),
            pltpu.VMEM((rows, TILE), jnp.float32),
            layered,
            layered,
            flat,
            layered,
            pltpu.VMEM((blocks, groups, block), jnp.float32),
            pltpu.VMEM((LAYERS, peers, groups, block), jnp.float32),
            pltpu.VMEM((peers, groups, block), jnp.float32),
            small,
            pltpu.SemaphoreType.DMA((3,)),
            single,
            single,
            single,
            single,
            single,
            single,
            pltpu.SemaphoreType.DMA((3,)),
            single,
            by_group,
            by_group,
            single,
            single,
            pltpu.SemaphoreType.DMA((groups, LAYERS)),
            pltpu.SemaphoreType.DMA((groups, LAYERS)),
            single,
            by_layer,
            single,
            by_layer,
            pltpu.SemaphoreType.REGULAR((LAYERS,)),
        ],
        compiler_params=pltpu.CompilerParams(
            collective_id=0, has_side_effects=True, vmem_limit_bytes=VMEM_LIMIT
        ),
    )(inputs, gating, grad_out, filters)
    return pl.pallas_call(
        store_kernel,
        out_shape=outs,
        in_specs=[vmem] * 3,
        out_specs=(hbm, hbm, hbm),
        scratch_shapes=[pltpu.SemaphoreType.DMA((3,))],
        compiler_params=pltpu.CompilerParams(vmem_limit_bytes=1024 * 1024),
    )(*results)


VMEM_LIMIT = 53900 * 1024


def solution(mesh):
    placed = (P("chan", "seq"), P("chan", "seq"), P("chan", "seq"), P(None, ("seq", "chan")))
    layered = mesh.shape["seq"] == 16 and mesh.shape["chan"] == 2
    return jax.shard_map(
        layered_shards if layered else shards,
        mesh=mesh,
        in_specs=placed,
        out_specs=(P("chan", "seq"), P("chan", "seq"), P(None, ("seq", "chan"))),
        check_vma=False,
    )
```

```python
import functools
import math

import jax
import jax.numpy as jnp
from jax import lax
from jax.experimental import pallas as pl
from jax.experimental.pallas import tpu as pltpu
from jax.sharding import PartitionSpec as P

D = 4096
G = 64


HIGHEST = lax.Precision.HIGHEST


def make_tables(seq_count, block_len):
    outer = 2 * seq_count
    total = outer * block_len
    outer_index = jnp.arange(outer, dtype=jnp.int32)
    block_index = jnp.arange(seq_count, dtype=jnp.int32)
    inner_index = jnp.arange(block_len, dtype=jnp.int32)
    block_angle = (outer_index[:, None] * block_index[None, :] % outer).astype(jnp.float32) * (
        2.0 * math.pi / outer
    )
    twist_angle = (outer_index[:, None] * inner_index[None, :] % total).astype(jnp.float32) * (
        2.0 * math.pi / total
    )
    inner_angle = (inner_index[:, None] * inner_index[None, :] % block_len).astype(jnp.float32) * (
        2.0 * math.pi / block_len
    )
    return (
        jnp.cos(block_angle),
        jnp.sin(block_angle),
        jnp.cos(twist_angle),
        jnp.sin(twist_angle),
        jnp.cos(inner_angle),
        jnp.sin(inner_angle),
    )


def right_product(values, table):
    return jnp.einsum("ckm,mj->ckj", values, table, precision=HIGHEST)


def forward_dft(signal, tables):
    block_cos, block_sin, twist_cos, twist_sin, inner_cos, inner_sin = tables
    real_first = jnp.einsum("kn,cnm->ckm", block_cos, signal, precision=HIGHEST)
    imag_first = -jnp.einsum("kn,cnm->ckm", block_sin, signal, precision=HIGHEST)
    real_twist = real_first * twist_cos + imag_first * twist_sin
    imag_twist = imag_first * twist_cos - real_first * twist_sin
    real_spec = right_product(real_twist, inner_cos) + right_product(imag_twist, inner_sin)
    imag_spec = right_product(imag_twist, inner_cos) - right_product(real_twist, inner_sin)
    return (real_spec, imag_spec)


def inverse_dft(real_spec, imag_spec, tables):
    block_cos, block_sin, twist_cos, twist_sin, inner_cos, inner_sin = tables
    real_first = right_product(real_spec, inner_cos) - right_product(imag_spec, inner_sin)
    imag_first = right_product(real_spec, inner_sin) + right_product(imag_spec, inner_cos)
    real_twist = real_first * twist_cos - imag_first * twist_sin
    imag_twist = real_first * twist_sin + imag_first * twist_cos
    total = real_spec.shape[1] * real_spec.shape[2]
    result = jnp.einsum("kn,ckm->cnm", block_cos, real_twist, precision=HIGHEST)
    result = result - jnp.einsum("kn,ckm->cnm", block_sin, imag_twist, precision=HIGHEST)
    return result / total


def shards(inputs, gating, grad_out, filters):
    seq_count = lax.axis_size("seq")
    chan_count = lax.axis_size("chan")
    chan_rows, block_len = inputs.shape
    local_chan = chan_rows // seq_count
    group_width = D // G
    groups_here = G // chan_count
    local_groups = max(1, local_chan // group_width)
    group_share = local_chan // local_groups
    copies = max(1, seq_count // groups_here)
    length = block_len * seq_count
    outer = 2 * seq_count
    factor = 1.0 / math.sqrt(group_width * length)
    tables = make_tables(seq_count, block_len)
    whole = lax.all_gather(filters, ("seq", "chan"), axis=1, tiled=True)
    first_group = (
        lax.axis_index("chan") * chan_rows + lax.axis_index("seq") * local_chan
    ) // group_width
    kernel_rows = lax.dynamic_slice_in_dim(whole, first_group, local_groups, 0)
    kernel_blocks = kernel_rows.reshape(local_groups, seq_count, block_len)
    kernel_real, kernel_imag = forward_dft(kernel_blocks * factor, tables)
    kernel_real = kernel_real[:, None]
    kernel_imag = kernel_imag[:, None]
    shaped_inputs = inputs.reshape(chan_rows, 1, block_len)
    values, gate_part, upstream = (
        lax.all_to_all(shaped_inputs, "seq", split_axis=0, concat_axis=1, tiled=True),
        lax.all_to_all(
            gating.reshape(chan_rows, 1, block_len), "seq", split_axis=0, concat_axis=1, tiled=True
        ),
        lax.all_to_all(
            grad_out.reshape(chan_rows, 1, block_len),
            "seq",
            split_axis=0,
            concat_axis=1,
            tiled=True,
        ),
    )
    input_real, input_imag = forward_dft(values.astype(jnp.float32), tables)
    upstream_f = upstream.astype(jnp.float32)
    product_b = lax.optimization_barrier(
        (gate_part.astype(jnp.float32) * upstream_f).astype(jnp.bfloat16)
    )
    up_real, up_imag = forward_dft(product_b.astype(jnp.float32), tables)
    grouped_shape = (local_groups, group_share, outer, block_len)
    input_real = input_real.reshape(grouped_shape)
    input_imag = input_imag.reshape(grouped_shape)
    up_real = up_real.reshape(grouped_shape)
    up_imag = up_imag.reshape(grouped_shape)
    flat_shape = (local_chan, outer, block_len)
    conv_real = input_real * kernel_real - input_imag * kernel_imag
    conv_imag = input_real * kernel_imag + input_imag * kernel_real
    convolved = inverse_dft(conv_real.reshape(flat_shape), conv_imag.reshape(flat_shape), tables)
    conv_b = convolved.astype(jnp.bfloat16)
    second = (upstream_f * lax.optimization_barrier(conv_b).astype(jnp.float32)).astype(
        jnp.bfloat16
    )
    back_real = up_real * kernel_real + up_imag * kernel_imag
    back_imag = up_imag * kernel_real - up_real * kernel_imag
    grad_input = inverse_dft(
        back_real.reshape(flat_shape), back_imag.reshape(flat_shape), tables
    ).astype(jnp.bfloat16)
    returned_input, returned_second = (
        lax.all_to_all(grad_input, "seq", split_axis=1, concat_axis=0, tiled=True),
        lax.all_to_all(second, "seq", split_axis=1, concat_axis=0, tiled=True),
    )
    returned_second = returned_second.reshape(chan_rows, block_len)
    cross_real = jnp.sum(input_real * up_real + input_imag * up_imag, axis=1)
    cross_imag = jnp.sum(input_real * up_imag - input_imag * up_real, axis=1)
    partial_grad = inverse_dft(cross_real, cross_imag, tables) * factor
    received = lax.all_to_all(partial_grad, "seq", split_axis=1, concat_axis=0, tiled=True)
    summed = received.reshape(groups_here, copies, block_len).sum(axis=1)
    grad_filters = lax.all_to_all(summed, "chan", split_axis=1, concat_axis=0, tiled=True)
    return (returned_input.reshape(chan_rows, block_len), returned_second, grad_filters)


GROUP_WIDTH = D // G
MESH = pl.DeviceIdType.MESH
TILE = 256
LAYERS = 4
LEAD, DELAY_SECOND, DELAY_RELAY, DELAY_COMPUTE, DELAY_OUTER = 4, 1, 2, 3, 6
NT = (((1,), (1,)), ((), ()))
NN = (((1,), (0,)), ((), ()))


def dot(a, b, dims):
    return lax.dot_general(a, b, dims, preferred_element_type=jnp.float32)


def layered_kernel(
    seq_count,
    chan_count,
    x_hbm,
    gate_hbm,
    up_hbm,
    raw_hbm,
    gi_ref,
    gg_ref,
    grad_ref,
    gate_ref,
    up_ref,
    raw_ref,
    filt_ref,
    filt_in,
    filt_layer,
    filt_all,
    u_loc,
    xs,
    us,
    table,
    acc_c,
    acc_g,
    cv,
    gv,
    conv_in,
    far,
    fg_out,
    fg_layer,
    fg_sum,
    fg_in,
    load_sem,
    x_send,
    u_send,
    c_send,
    g_send,
    z_send,
    far_send,
    f_send,
    k_send,
    x_recv,
    u_recv,
    c_recv,
    g_recv,
    zx_recv,
    zu_recv,
    f_recv,
    fz_recv,
    k_recv,
    kz_recv,
    enter_sem,
):
    seq = lax.axis_index("seq")
    chan = lax.axis_index("chan")
    peers = seq_count // LAYERS
    crew = peers * chan_count
    layer = seq // peers
    spot = lax.rem(seq, peers)
    slot = spot * chan_count + chan
    last = LAYERS - 1
    groups = xs.shape[0]
    block = x_hbm.shape[1]
    per_tile = TILE // block
    length = block * seq_count
    tiles = length // TILE
    half = tiles // LAYERS
    width = GROUP_WIDTH
    layer_rows = half * width
    local_chan = groups * width
    share = raw_hbm.shape[1]
    factor = 1.0 / math.sqrt(width * length)

    loads = [
        pltpu.make_async_copy(gate_hbm, gate_ref, load_sem.at[0]),
        pltpu.make_async_copy(up_hbm, up_ref, load_sem.at[1]),
        pltpu.make_async_copy(raw_hbm, raw_ref, load_sem.at[2]),
    ]
    for load in loads:
        load.start()

    barrier = pltpu.get_barrier_semaphore()

    def greet(to_seq, to_chan):
        pl.semaphore_signal(barrier, inc=1, device_id=(to_seq, to_chan), device_id_type=MESH)

    def crew_member(k):
        other = lax.rem(slot + k, crew)
        return other // chan_count, lax.rem(other, chan_count)

    for k in range(1, crew):
        p, c = crew_member(k)
        greet(layer * peers + p, c)
    everyone, lone = range(peers), (spot,)
    greeted = {
        0: ((1, everyone), (2, lone)),
        1: ((0, lone), (2, lone), (3, lone)),
        2: ((0, lone), (1, lone), (3, everyone)),
        3: (),
    }
    for which in range(LAYERS):

        @pl.when(layer == which)
        def _(which=which):
            for to_layer, spots in greeted[which]:
                for p in spots:
                    greet(to_layer * peers + p, chan)

    fg_out[...] = jnp.zeros_like(fg_out)
    loads[2].wait()
    scaled = raw_ref[...] * factor
    lanes = jnp.concatenate([scaled] * chan_count, axis=1)
    kept = lax.broadcasted_iota(jnp.int32, lanes.shape, 1) // share == chan
    lanes = jnp.where(kept, lanes, 0.0)
    for i in range(crew):
        filt_ref[i] = lanes[i * groups : (i + 1) * groups, :]
    loads[0].wait()
    loads[1].wait()
    u_loc[...] = (
        gate_ref[...].astype(jnp.float32) * up_ref[...].astype(jnp.float32)
    ).astype(jnp.bfloat16)
    expected = {0: 2, 1: peers + 1, 2: 2, 3: 1 + peers}
    for which in range(LAYERS):

        @pl.when(layer == which)
        def _(which=which):
            pl.semaphore_wait(barrier, crew - 1 + expected[which])

    def enter(origin, to_layer, p):
        pl.semaphore_signal(
            enter_sem.at[origin],
            inc=1,
            device_id=(to_layer * peers + p, chan),
            device_id_type=MESH,
        )

    @pl.when(layer == 3)
    def _():
        for p in everyone:
            enter(3, 2, p)
        enter(3, 1, spot)

    def place(ref, g, s):
        return ref.at[
            g,
            pl.ds(pl.multiple_of((s // per_tile) * width, width), width),
            pl.ds(pl.multiple_of(lax.rem(s, per_tile) * block, block), block),
        ]

    def strip(ref, q, g):
        return ref.at[pl.ds(pl.multiple_of(q * local_chan + g * width, width), width), :]

    def remote(from_ref, to_ref, send, recv, to_seq, to_chan=None):
        return pltpu.make_async_remote_copy(
            src_ref=from_ref,
            dst_ref=to_ref,
            send_sem=send,
            recv_sem=recv,
            device_id=(to_seq, chan if to_chan is None else to_chan),
            device_id_type=MESH,
        )

    def wait_bytes(ref, sem):
        pltpu.make_async_copy(ref, ref, sem).wait()

    def layer_span(ref, g, which):
        return ref.at[g, pl.ds(pl.multiple_of(which * layer_rows, layer_rows), layer_rows), :]

    def scatter(ref, buf, send, recv, g):
        for k in (2, 3, 1):
            p = lax.rem(spot + k, peers)
            remote(
                strip(ref, p, g), place(buf, g, seq), send.at[0], recv.at[g], layer * peers + p
            ).start()
        pltpu.make_async_copy(strip(ref, spot, g), place(buf, g, seq), recv.at[g]).start()

    def mirror(g):
        return groups - 1 - g

    def scatter_both(g):
        @pl.when(layer < LAYERS // 2)
        def _():
            scatter(x_hbm, xs, x_send, x_recv, g)
            scatter(u_loc, us, u_send, u_recv, mirror(g))

        @pl.when(layer >= LAYERS // 2)
        def _():
            scatter(u_loc, us, u_send, u_recv, mirror(g))
            scatter(x_hbm, xs, x_send, x_recv, g)

    def give_back(buf, ref, send, recv, g):
        for k in (2, 3, 1):
            p = lax.rem(spot + k, peers)
            remote(
                place(buf, g, p), strip(ref, spot, g), send.at[0], recv.at[0], layer * peers + p
            ).start()
        pltpu.make_async_copy(place(buf, g, spot), strip(ref, spot, g), recv.at[0]).start()

    def send_far(g, ref, recv, to_layer):
        for k in (2, 3, 1, 0):
            p = lax.rem(spot + k, peers)
            remote(
                place(far, g, p), strip(ref, spot, g), far_send.at[0], recv.at[0],
                to_layer * peers + p,
            ).start()

    def hop_x(g, origin, to_layer):
        ref = layer_span(xs, g, origin)
        return remote(ref, ref, z_send.at[0], zx_recv.at[g, origin], to_layer * peers + spot)

    def hop_u(g, origin, to_layer):
        ref = layer_span(us, g, origin)
        return remote(ref, ref, z_send.at[0], zu_recv.at[g, origin], to_layer * peers + spot)

    def ahead(from_ref, buf, recv, origin, to_layer, order=lambda g: g):
        def step(i, carry):
            g = order(i)
            remote(
                strip(from_ref, spot, g), place(buf, g, seq), z_send.at[0], recv.at[g, origin],
                to_layer * peers + spot,
            ).start()
            return carry

        lax.fori_loop(0, groups, step, 0)

    def rest(g, buf, recv, origin, to_layer):
        sibling = spot + 1 - 2 * lax.rem(spot, per_tile)
        tile = origin * half + 1 - spot // per_tile
        refs = (
            place(buf, g, origin * peers + sibling),
            buf.at[g, pl.ds(pl.multiple_of(tile * width, width), width), :],
        )
        for ref in refs:
            remote(
                ref, ref, z_send.at[0], recv.at[g, origin], to_layer * peers + spot
            ).start()

    scatter_both(0)

    @pl.when(layer == 0)
    def _():
        ahead(x_hbm, xs, zx_recv, 0, 1)

    @pl.when(layer == 1)
    def _():
        ahead(x_hbm, xs, zx_recv, 1, 2)

    @pl.when(layer == 2)
    def _():
        ahead(u_loc, us, zu_recv, 2, 1, mirror)

    @pl.when(layer == 3)
    def _():
        ahead(u_loc, us, zu_recv, 3, 2, mirror)

    for k in range(1, crew):
        p, c = crew_member(k)
        remote(
            filt_ref.at[c * peers + p], filt_in.at[slot], k_send.at[0], k_recv.at[0],
            layer * peers + p, c,
        ).start()
    pltpu.make_async_copy(filt_ref.at[chan * peers + spot], filt_in.at[slot], k_recv.at[0]).start()

    def scatter_early(g, carry):
        scatter_both(g)
        return carry

    lax.fori_loop(1, LEAD, scatter_early, 0)

    filt_targets = {0: (1, 2), 1: (2,), 2: (1,), 3: (1, 2)}
    filt_sources = {0: (), 1: (0, 2, 3), 2: (0, 1, 3), 3: (0,)}

    def filt_hop(origin, to_layer):
        return remote(
            filt_layer.at[origin], filt_layer.at[origin], f_send.at[1], kz_recv.at[origin],
            to_layer * peers + spot,
        )

    def spread_filters():
        wait_bytes(filt_in, k_recv.at[0])
        parts = []
        for s in range(peers):
            part = filt_in[s * chan_count]
            for c in range(1, chan_count):
                part = part + filt_in[s * chan_count + c]
            parts.append(part)
        for s in range(peers // 2):
            pair = jnp.concatenate(parts[2 * s : 2 * s + 2], axis=0)
            filt_layer[layer, s] = pair.astype(jnp.bfloat16)
        for which in range(LAYERS):

            @pl.when(layer == which)
            def _(which=which):
                for to in filt_targets[which]:
                    filt_hop(which, to).start()

    def wait_x(g):
        wait_bytes(layer_span(xs, g, layer), x_recv.at[g])

    def wait_u(g):
        wait_bytes(layer_span(us, g, layer), u_recv.at[g])

    def gather_layer(g):
        @pl.when(layer == 0)
        def _():
            wait_x(g)
            rest(g, xs, zx_recv, 0, 1)

        @pl.when(layer == 1)
        def _():
            wait_x(g)
            rest(g, xs, zx_recv, 1, 2)

        @pl.when(layer == 2)
        def _():
            wait_u(mirror(g))
            rest(mirror(g), us, zu_recv, 2, 1)

        @pl.when(layer == 3)
        def _():
            wait_u(mirror(g))
            rest(mirror(g), us, zu_recv, 3, 2)

        @pl.when(g == 0)
        def _():
            spread_filters()

    def second(g):
        @pl.when(layer == 0)
        def _():
            wait_u(mirror(g))
            hop_u(mirror(g), 0, 1).start()

        @pl.when(layer == 3)
        def _():
            wait_x(g)
            hop_x(g, 3, 2).start()

    def relay(g):
        @pl.when(layer == 1)
        def _():
            hop_x(g, 0, 1).wait_recv()
            hop_x(g, 0, 2).start()

        @pl.when(layer == 2)
        def _():
            hop_u(mirror(g), 3, 2).wait_recv()
            hop_u(mirror(g), 3, 1).start()

    row_id = lax.broadcasted_iota(jnp.int32, (TILE, TILE), 0)
    col_id = lax.broadcasted_iota(jnp.int32, (TILE, TILE), 1)
    flip = jnp.where(row_id + col_id == TILE - 1, 1.0, 0.0).astype(jnp.bfloat16)
    row_in = lax.broadcasted_iota(jnp.int32, (block, block), 0)
    col_in = lax.broadcasted_iota(jnp.int32, (block, block), 1)
    upper = col_in >= row_in
    lower_flipped = col_in + row_in >= block - 1

    def compute(g, layers):
        for which in layers:

            @pl.when(layer == which)
            def _(which=which):
                compute_for(which, g)

    def span(first, final):
        return slice(first * width, (final + 1) * width)

    def make_table(g, lags):
        before = jnp.zeros((block, block), jnp.float32)
        for m in range(per_tile * lags):
            row = filt_all[m // peers, m % peers, pl.ds(g, 1), :]
            rolled = pltpu.roll(
                jnp.broadcast_to(row, (block, block)), 0, 1, stride=1, stride_axis=0
            )
            table[m] = jnp.where(upper, rolled, before).astype(jnp.bfloat16)
            before = rolled

    def filter_of(lag):
        rows = []
        for i in range(per_tile):
            parts = []
            for j in range(per_tile):
                m = lag * per_tile + j - i
                parts.append(table[m] if m >= 0 else jnp.zeros((block, block), jnp.bfloat16))
            rows.append(jnp.concatenate(parts, axis=1))
        return jnp.concatenate(rows, axis=0)

    def add(acc, seen, first, final, value):
        runs = []
        for tile in range(first, final + 1):
            if runs and runs[-1][2] == (tile in seen):
                runs[-1][1] = tile
            else:
                runs.append([tile, tile, tile in seen])
        for begin, end, known in runs:
            part = value[(begin - first) * width : (end - first + 1) * width]
            if known:
                acc[span(begin, end), :] += part
            else:
                acc[span(begin, end), :] = part
        seen.update(range(first, final + 1))

    def convolve(g, x_tiles, out_tiles):
        seen = set()
        for lag in range(out_tiles[1] - x_tiles[0] + 1):
            first = max(x_tiles[0], out_tiles[0] - lag)
            final = min(x_tiles[1], out_tiles[1] - lag)
            if first <= final:
                add(
                    acc_c, seen, first + lag, final + lag,
                    dot(xs[g, span(first, final), :], filter_of(lag), NN),
                )

    def correlate(g, u_tiles, out_tiles):
        seen = set()
        for lag in range(u_tiles[1] - out_tiles[0] + 1):
            first = max(u_tiles[0], out_tiles[0] + lag)
            final = min(u_tiles[1], out_tiles[1] + lag)
            if first <= final:
                add(
                    acc_g, seen, first - lag, final - lag,
                    dot(us[g, span(first, final), :], filter_of(lag), NT),
                )

    def filter_grad(g, x_tiles, u_tiles):
        turned = {}

        def turned_from(tile):
            if tile not in turned:
                rows = xs[g, span(tile, x_tiles[1]), :]
                turned[tile] = dot(flip, rows, NT).astype(jnp.bfloat16)
            return turned[tile]

        def gram_of(lag):
            first = max(x_tiles[0], u_tiles[0] - lag)
            final = min(x_tiles[1], u_tiles[1] - lag)
            base = x_tiles[0] + (first - x_tiles[0]) % per_tile
            left = turned_from(base)[:, (first - base) * width : (final + 1 - base) * width]
            return dot(left, us[g, span(first + lag, final + lag), :], NN)

        lags = u_tiles[1] - x_tiles[0] + 1
        zero = jnp.zeros((block, block), jnp.float32)
        gram = gram_of(0)
        current = gram[block:, :block] + gram[:block, block:]
        for lag in range(lags):
            following = gram_of(lag + 1) if lag + 1 < lags else None
            odd = gram[block:, block:]
            if following is None:
                even = zero
            else:
                odd = odd + following[:block, :block]
                even = following[block:, :block] + following[:block, block:]
            for i, (a, b) in enumerate(((current, odd), (odd, even))):
                mixed = jnp.where(lower_flipped, a, b)
                aligned = pltpu.roll(mixed, 1, 1, stride=1, stride_axis=0)
                total = jnp.sum(aligned, axis=0, keepdims=True) * factor
                fg_out[lag * per_tile + i, pl.ds(g, 1), :] = total
            current, gram = even, following

    def send_grads(g, which):
        @pl.when(g == groups - 1)
        def _():
            if which == 1:
                pl.semaphore_wait(enter_sem.at[3], 1)
            for to in grad_targets[which]:
                grad_hop(which, to).start()

    def back_conv(g, tile):
        cv[g] = acc_c[span(tile, tile + half - 1), :].astype(jnp.bfloat16)
        give_back(cv, conv_in, c_send, c_recv, g)

    def back_grad(g, tile):
        gv[g] = acc_g[span(tile, tile + half - 1), :].astype(jnp.bfloat16)
        give_back(gv, gi_ref, g_send, g_recv, g)

    def compute_for(which, g):
        low, high = which * half, (which + 1) * half - 1

        @pl.when(g == 0)
        def _():
            for origin in filt_sources[which]:
                filt_hop(origin, which).wait_recv()
            if which == 2:
                pl.semaphore_wait(enter_sem.at[3], peers)
                filt_hop(0, 3).start()
            for origin in sorted(filt_sources[which] + ((which,) if which < last else ())):
                filt_all[origin] = (
                    filt_layer[origin].astype(jnp.float32).reshape(peers, groups, block)
                )

        other = mirror(g)
        if which == 0:
            make_table(g, half)
            convolve(g, (low, high), (low, high))
            back_conv(g, low)
        if which == 1:
            make_table(g, 2 * half)
            convolve(g, (0, high), (low, high))
            back_conv(g, low)
            wait_u(other)
            hop_u(other, 0, 1).wait_recv()

            @pl.when(g >= groups // 2)
            def _():
                filter_grad(g, (0, high), (0, tiles - 1))
                filter_grad(other, (0, high), (0, high))

            send_grads(g, which)
            make_table(other, tiles)
            hop_u(other, 2, 1).wait_recv()
            hop_u(other, 3, 1).wait_recv()
            correlate(other, (0, tiles - 1), (0, high))
            far[other] = acc_g[span(0, low - 1), :].astype(jnp.bfloat16)
            send_far(other, gi_ref, g_recv, 0)
            back_grad(other, low)
        if which == 2:
            make_table(other, 2 * half)
            correlate(other, (low, tiles - 1), (low, high))
            back_grad(other, low)
            wait_x(g)
            hop_x(g, 3, 2).wait_recv()

            @pl.when(g >= groups // 2)
            def _():
                filter_grad(other, (0, tiles - 1), (low, tiles - 1))
                filter_grad(g, (low, tiles - 1), (low, tiles - 1))

            send_grads(g, which)
            make_table(g, tiles)
            hop_x(g, 1, 2).wait_recv()
            hop_x(g, 0, 2).wait_recv()
            convolve(g, (0, tiles - 1), (low, tiles - 1))
            far[g] = acc_c[span(high + 1, tiles - 1), :].astype(jnp.bfloat16)
            send_far(g, conv_in, c_recv, 3)
            back_conv(g, low)
        if which == 3:
            make_table(other, half)
            correlate(other, (low, high), (low, high))
            back_grad(other, low)

    grad_targets = {0: (), 1: (0, 2, 3), 2: (0, 1, 3), 3: ()}
    grad_sources = {0: (1, 2), 1: (2,), 2: (1,), 3: (1, 2)}

    def grad_hop(origin, to_layer):
        return remote(
            fg_out.at[pl.ds(to_layer * peers, peers)], fg_layer.at[origin], f_send.at[0],
            fz_recv.at[origin], to_layer * peers + spot,
        )

    def stage(step, delay, body):
        @pl.when((step >= delay) & (step < groups + delay))
        def _():
            body(step - delay)

    def scatter_later(g):
        @pl.when(g >= LEAD)
        def _():
            scatter_both(g)

    def pipeline(step, carry):
        stage(step, 0, gather_layer)
        stage(step, -LEAD, scatter_later)
        stage(step, DELAY_SECOND, second)
        stage(step, DELAY_RELAY, relay)
        stage(step, DELAY_COMPUTE, lambda g: compute(g, (1, 2)))
        stage(step, DELAY_OUTER, lambda g: compute(g, (0, last)))
        return carry

    lax.fori_loop(0, groups + DELAY_OUTER, pipeline, 0)

    for which in range(LAYERS):

        @pl.when(layer == which)
        def _(which=which):
            total = None
            if which in (1, 2):
                total = fg_out[which * peers : (which + 1) * peers]
            for origin in grad_sources[which]:
                grad_hop(origin, which).wait_recv()
                part = fg_layer[origin]
                total = part if total is None else total + part
            fg_sum[...] = total

    for k in range(1, crew):
        p, c = crew_member(k)
        remote(
            fg_sum.at[p], fg_in.at[chan * peers + spot], f_send.at[2], f_recv.at[0],
            layer * peers + p, c,
        ).start()
    pltpu.make_async_copy(fg_sum.at[spot], fg_in.at[chan * peers + spot], f_recv.at[0]).start()

    wait_bytes(conv_in, c_recv.at[0])
    gg_ref[...] = (up_ref[...].astype(jnp.float32) * conv_in[...].astype(jnp.float32)).astype(
        jnp.bfloat16
    )
    wait_bytes(gi_ref, g_recv.at[0])
    wait_bytes(fg_in, f_recv.at[0])
    for i in range(crew):
        total = fg_in[i]
        kept_part = total[:, :share]
        for d in range(1, chan_count):
            kept_part = jnp.where(chan == d, total[:, d * share : (d + 1) * share], kept_part)
        grad_ref[i * groups : (i + 1) * groups, :] = kept_part

    sent = pl.ds(0, groups * (peers - 1) // peers)
    wait_bytes(cv.at[sent], x_send.at[0])
    wait_bytes(cv.at[sent], u_send.at[0])
    wait_bytes(filt_in.at[pl.ds(0, crew - 1)], k_send.at[0])
    wait_bytes(filt_in.at[pl.ds(0, crew - 1)], f_send.at[2])
    wait_bytes(cv, z_send.at[0])
    wait_bytes(cv, z_send.at[0])
    for which in range(LAYERS):

        @pl.when(layer == which)
        def _(which=which):
            if which < last:
                wait_bytes(cv.at[sent], c_send.at[0])
            if which > 0:
                wait_bytes(cv.at[sent], g_send.at[0])
            if which in (1, 2):
                wait_bytes(cv, far_send.at[0])
            for _ in filt_targets[which] + ((3,) if which == 2 else ()):
                wait_bytes(filt_layer.at[0], f_send.at[1])
            for _ in grad_targets[which]:
                wait_bytes(fg_layer.at[0], f_send.at[0])


def store_kernel(a_ref, b_ref, c_ref, a_out, b_out, c_out, sems):
    copies = [
        pltpu.make_async_copy(a_ref, a_out, sems.at[0]),
        pltpu.make_async_copy(b_ref, b_out, sems.at[1]),
        pltpu.make_async_copy(c_ref, c_out, sems.at[2]),
    ]
    for copy in copies:
        copy.start()
    for copy in copies:
        copy.wait()


def layered_shards(inputs, gating, grad_out, filters):
    seq_count = lax.axis_size("seq")
    chan_count = lax.axis_size("chan")
    chan_rows, block = inputs.shape
    peers = seq_count // LAYERS
    crew = peers * chan_count
    groups = chan_rows // peers // GROUP_WIDTH
    length = block * seq_count
    tiles = length // TILE
    rows = tiles * GROUP_WIDTH
    layer_rows = rows // LAYERS
    blocks = length // block
    vmem = pl.BlockSpec(memory_space=pltpu.VMEM)
    hbm = pl.BlockSpec(memory_space=pltpu.HBM)
    single = pltpu.SemaphoreType.DMA((1,))
    by_group = pltpu.SemaphoreType.DMA((groups,))
    by_layer = pltpu.SemaphoreType.DMA((LAYERS,))
    flat = pltpu.VMEM((chan_rows, block), jnp.bfloat16)
    layered = pltpu.VMEM((groups, layer_rows, TILE), jnp.bfloat16)
    small = pltpu.VMEM((crew, groups, block), jnp.float32)
    outs = (
        jax.ShapeDtypeStruct((chan_rows, block), jnp.bfloat16),
        jax.ShapeDtypeStruct((chan_rows, block), jnp.bfloat16),
        jax.ShapeDtypeStruct(filters.shape, jnp.float32),
    )
    results = pl.pallas_call(
        functools.partial(layered_kernel, seq_count, chan_count),
        out_shape=outs,
        in_specs=[hbm] * 4,
        out_specs=(vmem, vmem, vmem),
        scratch_shapes=[
            flat,
            flat,
            pltpu.VMEM(filters.shape, jnp.float32),
            small,
            small,
            pltpu.VMEM((LAYERS, peers // 2, 2 * groups, block), jnp.bfloat16),
            pltpu.VMEM((LAYERS, peers, groups, block), jnp.float32),
            flat,
            pltpu.VMEM((groups, rows, TILE), jnp.bfloat16),
            pltpu.VMEM((groups, rows, TILE), jnp.bfloat16),
            pltpu.VMEM((blocks, block, block), jnp.bfloat16),
            pltpu.VMEM((rows, TILE), jnp.float32),
            pltpu.VMEM((rows, TILE), jnp.float32),
            layered,
            layered,
            flat,
            layered,
            pltpu.VMEM((blocks, groups, block), jnp.float32),
            pltpu.VMEM((LAYERS, peers, groups, block), jnp.float32),
            pltpu.VMEM((peers, groups, block), jnp.float32),
            small,
            pltpu.SemaphoreType.DMA((3,)),
            single,
            single,
            single,
            single,
            single,
            single,
            pltpu.SemaphoreType.DMA((3,)),
            single,
            by_group,
            by_group,
            single,
            single,
            pltpu.SemaphoreType.DMA((groups, LAYERS)),
            pltpu.SemaphoreType.DMA((groups, LAYERS)),
            single,
            by_layer,
            single,
            by_layer,
            pltpu.SemaphoreType.REGULAR((LAYERS,)),
        ],
        compiler_params=pltpu.CompilerParams(
            collective_id=0, has_side_effects=True, vmem_limit_bytes=VMEM_LIMIT
        ),
    )(inputs, gating, grad_out, filters)
    return pl.pallas_call(
        store_kernel,
        out_shape=outs,
        in_specs=[vmem] * 3,
        out_specs=(hbm, hbm, hbm),
        scratch_shapes=[pltpu.SemaphoreType.DMA((3,))],
        compiler_params=pltpu.CompilerParams(vmem_limit_bytes=1024 * 1024),
    )(*results)


VMEM_LIMIT = 53900 * 1024


def solution(mesh):
    placed = (P("chan", "seq"), P("chan", "seq"), P("chan", "seq"), P(None, ("seq", "chan")))
    layered = mesh.shape["seq"] == 16 and mesh.shape["chan"] == 2
    return jax.shard_map(
        layered_shards if layered else shards,
        mesh=mesh,
        in_specs=placed,
        out_specs=(P("chan", "seq"), P("chan", "seq"), P(None, ("seq", "chan"))),
        check_vma=False,
    )
```

```python
import functools
import math

import jax
import jax.numpy as jnp
from jax import lax
from jax.experimental import pallas as pl
from jax.experimental.pallas import tpu as pltpu
from jax.sharding import PartitionSpec as P

D = 4096
G = 64


HIGHEST = lax.Precision.HIGHEST


def make_tables(seq_count, block_len):
    outer = 2 * seq_count
    total = outer * block_len
    outer_index = jnp.arange(outer, dtype=jnp.int32)
    block_index = jnp.arange(seq_count, dtype=jnp.int32)
    inner_index = jnp.arange(block_len, dtype=jnp.int32)
    block_angle = (outer_index[:, None] * block_index[None, :] % outer).astype(jnp.float32) * (
        2.0 * math.pi / outer
    )
    twist_angle = (outer_index[:, None] * inner_index[None, :] % total).astype(jnp.float32) * (
        2.0 * math.pi / total
    )
    inner_angle = (inner_index[:, None] * inner_index[None, :] % block_len).astype(jnp.float32) * (
        2.0 * math.pi / block_len
    )
    return (
        jnp.cos(block_angle),
        jnp.sin(block_angle),
        jnp.cos(twist_angle),
        jnp.sin(twist_angle),
        jnp.cos(inner_angle),
        jnp.sin(inner_angle),
    )


def right_product(values, table):
    return jnp.einsum("ckm,mj->ckj", values, table, precision=HIGHEST)


def forward_dft(signal, tables):
    block_cos, block_sin, twist_cos, twist_sin, inner_cos, inner_sin = tables
    real_first = jnp.einsum("kn,cnm->ckm", block_cos, signal, precision=HIGHEST)
    imag_first = -jnp.einsum("kn,cnm->ckm", block_sin, signal, precision=HIGHEST)
    real_twist = real_first * twist_cos + imag_first * twist_sin
    imag_twist = imag_first * twist_cos - real_first * twist_sin
    real_spec = right_product(real_twist, inner_cos) + right_product(imag_twist, inner_sin)
    imag_spec = right_product(imag_twist, inner_cos) - right_product(real_twist, inner_sin)
    return (real_spec, imag_spec)


def inverse_dft(real_spec, imag_spec, tables):
    block_cos, block_sin, twist_cos, twist_sin, inner_cos, inner_sin = tables
    real_first = right_product(real_spec, inner_cos) - right_product(imag_spec, inner_sin)
    imag_first = right_product(real_spec, inner_sin) + right_product(imag_spec, inner_cos)
    real_twist = real_first * twist_cos - imag_first * twist_sin
    imag_twist = real_first * twist_sin + imag_first * twist_cos
    total = real_spec.shape[1] * real_spec.shape[2]
    result = jnp.einsum("kn,ckm->cnm", block_cos, real_twist, precision=HIGHEST)
    result = result - jnp.einsum("kn,ckm->cnm", block_sin, imag_twist, precision=HIGHEST)
    return result / total


def shards(inputs, gating, grad_out, filters):
    seq_count = lax.axis_size("seq")
    chan_count = lax.axis_size("chan")
    chan_rows, block_len = inputs.shape
    local_chan = chan_rows // seq_count
    group_width = D // G
    groups_here = G // chan_count
    local_groups = max(1, local_chan // group_width)
    group_share = local_chan // local_groups
    copies = max(1, seq_count // groups_here)
    length = block_len * seq_count
    outer = 2 * seq_count
    factor = 1.0 / math.sqrt(group_width * length)
    tables = make_tables(seq_count, block_len)
    whole = lax.all_gather(filters, ("seq", "chan"), axis=1, tiled=True)
    first_group = (
        lax.axis_index("chan") * chan_rows + lax.axis_index("seq") * local_chan
    ) // group_width
    kernel_rows = lax.dynamic_slice_in_dim(whole, first_group, local_groups, 0)
    kernel_blocks = kernel_rows.reshape(local_groups, seq_count, block_len)
    kernel_real, kernel_imag = forward_dft(kernel_blocks * factor, tables)
    kernel_real = kernel_real[:, None]
    kernel_imag = kernel_imag[:, None]
    shaped_inputs = inputs.reshape(chan_rows, 1, block_len)
    values, gate_part, upstream = (
        lax.all_to_all(shaped_inputs, "seq", split_axis=0, concat_axis=1, tiled=True),
        lax.all_to_all(
            gating.reshape(chan_rows, 1, block_len), "seq", split_axis=0, concat_axis=1, tiled=True
        ),
        lax.all_to_all(
            grad_out.reshape(chan_rows, 1, block_len),
            "seq",
            split_axis=0,
            concat_axis=1,
            tiled=True,
        ),
    )
    input_real, input_imag = forward_dft(values.astype(jnp.float32), tables)
    upstream_f = upstream.astype(jnp.float32)
    product_b = lax.optimization_barrier(
        (gate_part.astype(jnp.float32) * upstream_f).astype(jnp.bfloat16)
    )
    up_real, up_imag = forward_dft(product_b.astype(jnp.float32), tables)
    grouped_shape = (local_groups, group_share, outer, block_len)
    input_real = input_real.reshape(grouped_shape)
    input_imag = input_imag.reshape(grouped_shape)
    up_real = up_real.reshape(grouped_shape)
    up_imag = up_imag.reshape(grouped_shape)
    flat_shape = (local_chan, outer, block_len)
    conv_real = input_real * kernel_real - input_imag * kernel_imag
    conv_imag = input_real * kernel_imag + input_imag * kernel_real
    convolved = inverse_dft(conv_real.reshape(flat_shape), conv_imag.reshape(flat_shape), tables)
    conv_b = convolved.astype(jnp.bfloat16)
    second = (upstream_f * lax.optimization_barrier(conv_b).astype(jnp.float32)).astype(
        jnp.bfloat16
    )
    back_real = up_real * kernel_real + up_imag * kernel_imag
    back_imag = up_imag * kernel_real - up_real * kernel_imag
    grad_input = inverse_dft(
        back_real.reshape(flat_shape), back_imag.reshape(flat_shape), tables
    ).astype(jnp.bfloat16)
    returned_input, returned_second = (
        lax.all_to_all(grad_input, "seq", split_axis=1, concat_axis=0, tiled=True),
        lax.all_to_all(second, "seq", split_axis=1, concat_axis=0, tiled=True),
    )
    returned_second = returned_second.reshape(chan_rows, block_len)
    cross_real = jnp.sum(input_real * up_real + input_imag * up_imag, axis=1)
    cross_imag = jnp.sum(input_real * up_imag - input_imag * up_real, axis=1)
    partial_grad = inverse_dft(cross_real, cross_imag, tables) * factor
    received = lax.all_to_all(partial_grad, "seq", split_axis=1, concat_axis=0, tiled=True)
    summed = received.reshape(groups_here, copies, block_len).sum(axis=1)
    grad_filters = lax.all_to_all(summed, "chan", split_axis=1, concat_axis=0, tiled=True)
    return (returned_input.reshape(chan_rows, block_len), returned_second, grad_filters)


GROUP_WIDTH = D // G
MESH = pl.DeviceIdType.MESH
TILE = 256
LAYERS = 4
LEAD, DELAY_SECOND, DELAY_RELAY, DELAY_COMPUTE, DELAY_OUTER = 4, 1, 2, 3, 6
NT = (((1,), (1,)), ((), ()))
NN = (((1,), (0,)), ((), ()))


def dot(a, b, dims):
    return lax.dot_general(a, b, dims, preferred_element_type=jnp.float32)


def layered_kernel(
    seq_count,
    chan_count,
    x_hbm,
    gate_hbm,
    up_hbm,
    raw_hbm,
    gi_ref,
    gg_ref,
    grad_ref,
    gate_ref,
    up_ref,
    raw_ref,
    filt_ref,
    filt_in,
    filt_layer,
    filt_all,
    u_loc,
    xs,
    us,
    table,
    acc_c,
    acc_g,
    cv,
    gv,
    conv_in,
    far,
    fg_out,
    fg_in,
    load_sem,
    x_send,
    u_send,
    c_send,
    g_send,
    z_send,
    far_send,
    f_send,
    k_send,
    x_recv,
    u_recv,
    c_recv,
    g_recv,
    zx_recv,
    zu_recv,
    f_recv,
    k_recv,
    kz_recv,
    enter_sem,
):
    seq = lax.axis_index("seq")
    chan = lax.axis_index("chan")
    peers = seq_count // LAYERS
    crew = peers * chan_count
    layer = seq // peers
    spot = lax.rem(seq, peers)
    slot = spot * chan_count + chan
    last = LAYERS - 1
    groups = xs.shape[0]
    block = x_hbm.shape[1]
    per_tile = TILE // block
    length = block * seq_count
    tiles = length // TILE
    half = tiles // LAYERS
    width = GROUP_WIDTH
    layer_rows = half * width
    local_chan = groups * width
    share = raw_hbm.shape[1]
    factor = 1.0 / math.sqrt(width * length)

    loads = [
        pltpu.make_async_copy(gate_hbm, gate_ref, load_sem.at[0]),
        pltpu.make_async_copy(up_hbm, up_ref, load_sem.at[1]),
        pltpu.make_async_copy(raw_hbm, raw_ref, load_sem.at[2]),
    ]
    for load in loads:
        load.start()

    barrier = pltpu.get_barrier_semaphore()

    def greet(to_seq, to_chan):
        pl.semaphore_signal(barrier, inc=1, device_id=(to_seq, to_chan), device_id_type=MESH)

    def crew_member(k):
        other = lax.rem(slot + k, crew)
        return other // chan_count, lax.rem(other, chan_count)

    for k in range(1, crew):
        p, c = crew_member(k)
        greet(layer * peers + p, c)
    everyone = [(p, c) for p in range(peers) for c in range(chan_count)]
    lone = [(spot, chan)]
    greeted = {
        0: ((1, everyone), (2, everyone)),
        1: ((0, lone), (2, everyone), (3, everyone)),
        2: ((0, lone), (1, everyone), (3, everyone)),
        3: (),
    }
    for which in range(LAYERS):

        @pl.when(layer == which)
        def _(which=which):
            for to_layer, spots in greeted[which]:
                for p, c in spots:
                    greet(to_layer * peers + p, c)

    fg_out[...] = jnp.zeros_like(fg_out)
    loads[2].wait()
    scaled = raw_ref[...] * factor
    lanes = jnp.concatenate([scaled] * chan_count, axis=1)
    kept = lax.broadcasted_iota(jnp.int32, lanes.shape, 1) // share == chan
    lanes = jnp.where(kept, lanes, 0.0)
    for i in range(crew):
        filt_ref[i] = lanes[i * groups : (i + 1) * groups, :]
    loads[0].wait()
    loads[1].wait()
    u_loc[...] = (
        gate_ref[...].astype(jnp.float32) * up_ref[...].astype(jnp.float32)
    ).astype(jnp.bfloat16)
    expected = {0: 2, 1: 2 * crew, 2: 2 * crew, 3: 2 * crew}
    for which in range(LAYERS):

        @pl.when(layer == which)
        def _(which=which):
            pl.semaphore_wait(barrier, crew - 1 + expected[which])

    def enter(origin, to_layer, p, c):
        pl.semaphore_signal(
            enter_sem.at[origin],
            inc=1,
            device_id=(to_layer * peers + p, c),
            device_id_type=MESH,
        )

    @pl.when(layer == 3)
    def _():
        for p, c in everyone:
            enter(3, 2, p, c)
            enter(3, 1, p, c)

    def place(ref, g, s):
        return ref.at[
            g,
            pl.ds(pl.multiple_of((s // per_tile) * width, width), width),
            pl.ds(pl.multiple_of(lax.rem(s, per_tile) * block, block), block),
        ]

    def strip(ref, q, g):
        return ref.at[pl.ds(pl.multiple_of(q * local_chan + g * width, width), width), :]

    def remote(from_ref, to_ref, send, recv, to_seq, to_chan=None):
        return pltpu.make_async_remote_copy(
            src_ref=from_ref,
            dst_ref=to_ref,
            send_sem=send,
            recv_sem=recv,
            device_id=(to_seq, chan if to_chan is None else to_chan),
            device_id_type=MESH,
        )

    def wait_bytes(ref, sem):
        pltpu.make_async_copy(ref, ref, sem).wait()

    def layer_span(ref, g, which):
        return ref.at[g, pl.ds(pl.multiple_of(which * layer_rows, layer_rows), layer_rows), :]

    def scatter(ref, buf, send, recv, g):
        for k in (2, 3, 1):
            p = lax.rem(spot + k, peers)
            remote(
                strip(ref, p, g), place(buf, g, seq), send.at[0], recv.at[g], layer * peers + p
            ).start()
        pltpu.make_async_copy(strip(ref, spot, g), place(buf, g, seq), recv.at[g]).start()

    def mirror(g):
        return g + 1 - 2 * lax.rem(g, 2)

    def scatter_both(g):
        @pl.when(layer < LAYERS // 2)
        def _():
            scatter(x_hbm, xs, x_send, x_recv, g)
            scatter(u_loc, us, u_send, u_recv, mirror(g))

        @pl.when(layer >= LAYERS // 2)
        def _():
            scatter(u_loc, us, u_send, u_recv, mirror(g))
            scatter(x_hbm, xs, x_send, x_recv, g)

    def give_back(buf, ref, send, recv, g):
        for k in (2, 3, 1):
            p = lax.rem(spot + k, peers)
            remote(
                place(buf, g, p), strip(ref, spot, g), send.at[0], recv.at[0], layer * peers + p
            ).start()
        pltpu.make_async_copy(place(buf, g, spot), strip(ref, spot, g), recv.at[0]).start()

    def send_far(g, ref, recv, to_layer):
        for k in (2, 3, 1, 0):
            p = lax.rem(spot + k, peers)
            remote(
                place(far, g, p), strip(ref, spot, g), far_send.at[0], recv.at[0],
                to_layer * peers + p,
            ).start()

    def hop_x(g, origin, to_layer):
        ref = layer_span(xs, g, origin)
        return remote(ref, ref, z_send.at[0], zx_recv.at[g, origin], to_layer * peers + spot)

    def hop_u(g, origin, to_layer):
        ref = layer_span(us, g, origin)
        return remote(ref, ref, z_send.at[0], zu_recv.at[g, origin], to_layer * peers + spot)

    def ahead(from_ref, buf, recv, origin, to_layer, order=lambda g: g):
        def step(i, carry):
            g = order(i)
            remote(
                strip(from_ref, spot, g), place(buf, g, seq), z_send.at[0], recv.at[g, origin],
                to_layer * peers + spot,
            ).start()
            return carry

        lax.fori_loop(0, groups, step, 0)

    def rest(g, buf, recv, origin, to_layer):
        sibling = spot + 1 - 2 * lax.rem(spot, per_tile)
        tile = origin * half + 1 - spot // per_tile
        refs = (
            place(buf, g, origin * peers + sibling),
            buf.at[g, pl.ds(pl.multiple_of(tile * width, width), width), :],
        )
        for ref in refs:
            remote(
                ref, ref, z_send.at[0], recv.at[g, origin], to_layer * peers + spot
            ).start()

    scatter_both(0)

    @pl.when(layer == 0)
    def _():
        ahead(x_hbm, xs, zx_recv, 0, 1)

    @pl.when(layer == 1)
    def _():
        ahead(x_hbm, xs, zx_recv, 1, 2)

    @pl.when(layer == 2)
    def _():
        ahead(u_loc, us, zu_recv, 2, 1, mirror)

    @pl.when(layer == 3)
    def _():
        ahead(u_loc, us, zu_recv, 3, 2, mirror)

    for k in range(1, crew):
        p, c = crew_member(k)
        remote(
            filt_ref.at[c * peers + p], filt_in.at[slot], k_send.at[0], k_recv.at[0],
            layer * peers + p, c,
        ).start()
    pltpu.make_async_copy(filt_ref.at[chan * peers + spot], filt_in.at[slot], k_recv.at[0]).start()

    def scatter_early(g, carry):
        scatter_both(g)
        return carry

    lax.fori_loop(1, LEAD, scatter_early, 0)

    filt_targets = {0: (1, 2), 1: (2,), 2: (1,), 3: (1, 2)}
    filt_sources = {0: (), 1: (0, 2, 3), 2: (0, 1, 3), 3: (0,)}

    def filt_hop(origin, to_layer):
        return remote(
            filt_layer.at[origin], filt_layer.at[origin], f_send.at[1], kz_recv.at[origin],
            to_layer * peers + spot,
        )

    def spread_filters():
        wait_bytes(filt_in, k_recv.at[0])
        parts = []
        for s in range(peers):
            part = filt_in[s * chan_count]
            for c in range(1, chan_count):
                part = part + filt_in[s * chan_count + c]
            parts.append(part)
        for s in range(peers // 2):
            pair = jnp.concatenate(parts[2 * s : 2 * s + 2], axis=0)
            filt_layer[layer, s] = pair.astype(jnp.bfloat16)
        for which in range(LAYERS):

            @pl.when(layer == which)
            def _(which=which):
                for to in filt_targets[which]:
                    filt_hop(which, to).start()

    def wait_x(g):
        wait_bytes(layer_span(xs, g, layer), x_recv.at[g])

    def wait_u(g):
        wait_bytes(layer_span(us, g, layer), u_recv.at[g])

    def gather_layer(g):
        @pl.when(layer == 0)
        def _():
            wait_x(g)
            rest(g, xs, zx_recv, 0, 1)

        @pl.when(layer == 1)
        def _():
            wait_x(g)
            rest(g, xs, zx_recv, 1, 2)

        @pl.when(layer == 2)
        def _():
            wait_u(mirror(g))
            rest(mirror(g), us, zu_recv, 2, 1)

        @pl.when(layer == 3)
        def _():
            wait_u(mirror(g))
            rest(mirror(g), us, zu_recv, 3, 2)

        @pl.when(g == 0)
        def _():
            spread_filters()

    def second(g):
        @pl.when(layer == 0)
        def _():
            wait_u(mirror(g))
            hop_u(mirror(g), 0, 1).start()

        @pl.when(layer == 3)
        def _():
            wait_x(g)
            hop_x(g, 3, 2).start()

    def relay(g):
        @pl.when(layer == 1)
        def _():
            hop_x(g, 0, 1).wait_recv()
            hop_x(g, 0, 2).start()

        @pl.when(layer == 2)
        def _():
            hop_u(mirror(g), 3, 2).wait_recv()
            hop_u(mirror(g), 3, 1).start()

    row_id = lax.broadcasted_iota(jnp.int32, (TILE, TILE), 0)
    col_id = lax.broadcasted_iota(jnp.int32, (TILE, TILE), 1)
    flip = jnp.where(row_id + col_id == TILE - 1, 1.0, 0.0).astype(jnp.bfloat16)
    row_in = lax.broadcasted_iota(jnp.int32, (block, block), 0)
    col_in = lax.broadcasted_iota(jnp.int32, (block, block), 1)
    upper = col_in >= row_in
    lower_flipped = col_in + row_in >= block - 1

    def compute(g, layers):
        for which in layers:

            @pl.when(layer == which)
            def _(which=which):
                compute_for(which, g)

    def span(first, final):
        return slice(first * width, (final + 1) * width)

    def make_table(g, lags):
        before = jnp.zeros((block, block), jnp.float32)
        for m in range(per_tile * lags):
            row = filt_all[m // peers, m % peers, pl.ds(g, 1), :]
            rolled = pltpu.roll(
                jnp.broadcast_to(row, (block, block)), 0, 1, stride=1, stride_axis=0
            )
            table[m] = jnp.where(upper, rolled, before).astype(jnp.bfloat16)
            before = rolled

    def filter_of(lag):
        rows = []
        for i in range(per_tile):
            parts = []
            for j in range(per_tile):
                m = lag * per_tile + j - i
                parts.append(table[m] if m >= 0 else jnp.zeros((block, block), jnp.bfloat16))
            rows.append(jnp.concatenate(parts, axis=1))
        return jnp.concatenate(rows, axis=0)

    def add(acc, seen, first, final, value):
        runs = []
        for tile in range(first, final + 1):
            if runs and runs[-1][2] == (tile in seen):
                runs[-1][1] = tile
            else:
                runs.append([tile, tile, tile in seen])
        for begin, end, known in runs:
            part = value[(begin - first) * width : (end - first + 1) * width]
            if known:
                acc[span(begin, end), :] += part
            else:
                acc[span(begin, end), :] = part
        seen.update(range(first, final + 1))

    def convolve(g, x_tiles, out_tiles):
        seen = set()
        for lag in range(out_tiles[1] - x_tiles[0] + 1):
            first = max(x_tiles[0], out_tiles[0] - lag)
            final = min(x_tiles[1], out_tiles[1] - lag)
            if first <= final:
                add(
                    acc_c, seen, first + lag, final + lag,
                    dot(xs[g, span(first, final), :], filter_of(lag), NN),
                )

    def correlate(g, u_tiles, out_tiles):
        seen = set()
        for lag in range(u_tiles[1] - out_tiles[0] + 1):
            first = max(u_tiles[0], out_tiles[0] + lag)
            final = min(u_tiles[1], out_tiles[1] + lag)
            if first <= final:
                add(
                    acc_g, seen, first - lag, final - lag,
                    dot(us[g, span(first, final), :], filter_of(lag), NT),
                )

    def filter_grad(g, x_tiles, u_tiles):
        turned = {}

        def turned_from(tile):
            if tile not in turned:
                rows = xs[g, span(tile, x_tiles[1]), :]
                turned[tile] = dot(flip, rows, NT).astype(jnp.bfloat16)
            return turned[tile]

        def gram_of(lag):
            first = max(x_tiles[0], u_tiles[0] - lag)
            final = min(x_tiles[1], u_tiles[1] - lag)
            base = x_tiles[0] + (first - x_tiles[0]) % per_tile
            left = turned_from(base)[:, (first - base) * width : (final + 1 - base) * width]
            return dot(left, us[g, span(first + lag, final + lag), :], NN)

        lags = u_tiles[1] - x_tiles[0] + 1
        zero = jnp.zeros((block, block), jnp.float32)
        gram = gram_of(0)
        current = gram[block:, :block] + gram[:block, block:]
        for lag in range(lags):
            following = gram_of(lag + 1) if lag + 1 < lags else None
            odd = gram[block:, block:]
            if following is None:
                even = zero
            else:
                odd = odd + following[:block, :block]
                even = following[block:, :block] + following[:block, block:]
            for i, (a, b) in enumerate(((current, odd), (odd, even))):
                mixed = jnp.where(lower_flipped, a, b)
                aligned = pltpu.roll(mixed, 1, 1, stride=1, stride_axis=0)
                total = jnp.sum(aligned, axis=0, keepdims=True) * factor
                fg_out[lag * per_tile + i, pl.ds(g, 1), :] = total
            current, gram = even, following

    def send_grads(g, which):
        @pl.when(g == groups - 1)
        def _():
            if which == 1:
                pl.semaphore_wait(enter_sem.at[3], crew)
            for to in range(LAYERS):
                for k in range(1 if to == which else 0, crew):
                    p, c = crew_member(k)
                    remote(
                        fg_out.at[to * peers + p], fg_in.at[which, chan * peers + spot],
                        f_send.at[0], f_recv.at[which], to * peers + p, c,
                    ).start()
            pltpu.make_async_copy(
                fg_out.at[which * peers + spot], fg_in.at[which, chan * peers + spot],
                f_recv.at[which],
            ).start()

    def back_conv(g, tile):
        cv[g] = acc_c[span(tile, tile + half - 1), :].astype(jnp.bfloat16)
        give_back(cv, conv_in, c_send, c_recv, g)

    def back_grad(g, tile):
        gv[g] = acc_g[span(tile, tile + half - 1), :].astype(jnp.bfloat16)
        give_back(gv, gi_ref, g_send, g_recv, g)

    def compute_for(which, g):
        low, high = which * half, (which + 1) * half - 1

        @pl.when(g == 0)
        def _():
            for origin in filt_sources[which]:
                filt_hop(origin, which).wait_recv()
            if which == 2:
                pl.semaphore_wait(enter_sem.at[3], crew)
                filt_hop(0, 3).start()
            for origin in sorted(filt_sources[which] + ((which,) if which < last else ())):
                filt_all[origin] = (
                    filt_layer[origin].astype(jnp.float32).reshape(peers, groups, block)
                )

        other = mirror(g)
        odd = lax.rem(g, 2) == 1
        final = g == groups - 1
        own_step = (jnp.logical_not(odd) & (g > 0)) | final
        if which == 0:
            make_table(g, half)
            convolve(g, (low, high), (low, high))
            back_conv(g, low)
        if which == 1:
            make_table(g, 2 * half)
            convolve(g, (0, high), (low, high))
            back_conv(g, low)
            wait_u(other)
            hop_u(other, 0, 1).wait_recv()

            @pl.when(odd)
            def _():
                filter_grad(g, (0, high), (0, tiles - 1))

            @pl.when(own_step)
            def _():
                filter_grad(g - 2 + g // (groups - 1), (0, high), (0, high))

            send_grads(g, which)
            make_table(other, tiles)
            hop_u(other, 2, 1).wait_recv()
            hop_u(other, 3, 1).wait_recv()
            correlate(other, (0, tiles - 1), (0, high))
            far[other] = acc_g[span(0, low - 1), :].astype(jnp.bfloat16)
            send_far(other, gi_ref, g_recv, 0)
            back_grad(other, low)
        if which == 2:
            make_table(other, 2 * half)
            correlate(other, (low, tiles - 1), (low, high))
            back_grad(other, low)
            wait_x(g)
            hop_x(g, 3, 2).wait_recv()

            @pl.when(odd)
            def _():
                filter_grad(other, (0, tiles - 1), (low, tiles - 1))

            @pl.when(own_step)
            def _():
                filter_grad(g - 1 + g // (groups - 1), (low, tiles - 1), (low, tiles - 1))

            send_grads(g, which)
            make_table(g, tiles)
            hop_x(g, 1, 2).wait_recv()
            hop_x(g, 0, 2).wait_recv()
            convolve(g, (0, tiles - 1), (low, tiles - 1))
            far[g] = acc_c[span(high + 1, tiles - 1), :].astype(jnp.bfloat16)
            send_far(g, conv_in, c_recv, 3)
            back_conv(g, low)
        if which == 3:
            make_table(other, half)
            correlate(other, (low, high), (low, high))
            back_grad(other, low)

    def stage(step, delay, body):
        @pl.when((step >= delay) & (step < groups + delay))
        def _():
            body(step - delay)

    def scatter_later(g):
        @pl.when(g >= LEAD)
        def _():
            scatter_both(g)

    def pipeline(step, carry):
        stage(step, 0, gather_layer)
        stage(step, -LEAD, scatter_later)
        stage(step, DELAY_SECOND, second)
        stage(step, DELAY_RELAY, relay)
        stage(step, DELAY_COMPUTE, lambda g: compute(g, (1, 2)))
        stage(step, DELAY_OUTER, lambda g: compute(g, (0, last)))
        return carry

    lax.fori_loop(0, groups + DELAY_OUTER, pipeline, 0)

    wait_bytes(conv_in, c_recv.at[0])
    gg_ref[...] = (up_ref[...].astype(jnp.float32) * conv_in[...].astype(jnp.float32)).astype(
        jnp.bfloat16
    )
    wait_bytes(gi_ref, g_recv.at[0])
    wait_bytes(fg_in.at[1], f_recv.at[1])
    wait_bytes(fg_in.at[2], f_recv.at[2])
    for i in range(crew):
        total = fg_in[1, i] + fg_in[2, i]
        kept_part = total[:, :share]
        for d in range(1, chan_count):
            kept_part = jnp.where(chan == d, total[:, d * share : (d + 1) * share], kept_part)
        grad_ref[i * groups : (i + 1) * groups, :] = kept_part

    sent = pl.ds(0, groups * (peers - 1) // peers)
    wait_bytes(cv.at[sent], x_send.at[0])
    wait_bytes(cv.at[sent], u_send.at[0])
    wait_bytes(filt_in.at[pl.ds(0, crew - 1)], k_send.at[0])
    wait_bytes(cv, z_send.at[0])
    wait_bytes(cv, z_send.at[0])
    for which in range(LAYERS):

        @pl.when(layer == which)
        def _(which=which):
            if which < last:
                wait_bytes(cv.at[sent], c_send.at[0])
            if which > 0:
                wait_bytes(cv.at[sent], g_send.at[0])
            if which in (1, 2):
                wait_bytes(cv, far_send.at[0])
            for _ in filt_targets[which] + ((3,) if which == 2 else ()):
                wait_bytes(filt_layer.at[0], f_send.at[1])
            if which in (1, 2):
                for _ in range(LAYERS - 1):
                    wait_bytes(fg_in.at[0], f_send.at[0])
                wait_bytes(fg_in.at[0, pl.ds(0, crew - 1)], f_send.at[0])


def store_kernel(a_ref, b_ref, c_ref, a_out, b_out, c_out, sems):
    copies = [
        pltpu.make_async_copy(a_ref, a_out, sems.at[0]),
        pltpu.make_async_copy(b_ref, b_out, sems.at[1]),
        pltpu.make_async_copy(c_ref, c_out, sems.at[2]),
    ]
    for copy in copies:
        copy.start()
    for copy in copies:
        copy.wait()


def layered_shards(inputs, gating, grad_out, filters):
    seq_count = lax.axis_size("seq")
    chan_count = lax.axis_size("chan")
    chan_rows, block = inputs.shape
    peers = seq_count // LAYERS
    crew = peers * chan_count
    groups = chan_rows // peers // GROUP_WIDTH
    length = block * seq_count
    tiles = length // TILE
    rows = tiles * GROUP_WIDTH
    layer_rows = rows // LAYERS
    blocks = length // block
    vmem = pl.BlockSpec(memory_space=pltpu.VMEM)
    hbm = pl.BlockSpec(memory_space=pltpu.HBM)
    single = pltpu.SemaphoreType.DMA((1,))
    by_group = pltpu.SemaphoreType.DMA((groups,))
    by_layer = pltpu.SemaphoreType.DMA((LAYERS,))
    flat = pltpu.VMEM((chan_rows, block), jnp.bfloat16)
    layered = pltpu.VMEM((groups, layer_rows, TILE), jnp.bfloat16)
    small = pltpu.VMEM((crew, groups, block), jnp.float32)
    outs = (
        jax.ShapeDtypeStruct((chan_rows, block), jnp.bfloat16),
        jax.ShapeDtypeStruct((chan_rows, block), jnp.bfloat16),
        jax.ShapeDtypeStruct(filters.shape, jnp.float32),
    )
    results = pl.pallas_call(
        functools.partial(layered_kernel, seq_count, chan_count),
        out_shape=outs,
        in_specs=[hbm] * 4,
        out_specs=(vmem, vmem, vmem),
        scratch_shapes=[
            flat,
            flat,
            pltpu.VMEM(filters.shape, jnp.float32),
            small,
            small,
            pltpu.VMEM((LAYERS, peers // 2, 2 * groups, block), jnp.bfloat16),
            pltpu.VMEM((LAYERS, peers, groups, block), jnp.float32),
            flat,
            pltpu.VMEM((groups, rows, TILE), jnp.bfloat16),
            pltpu.VMEM((groups, rows, TILE), jnp.bfloat16),
            pltpu.VMEM((blocks, block, block), jnp.bfloat16),
            pltpu.VMEM((rows, TILE), jnp.float32),
            pltpu.VMEM((rows, TILE), jnp.float32),
            layered,
            layered,
            flat,
            layered,
            pltpu.VMEM((blocks, groups, block), jnp.float32),
            pltpu.VMEM((LAYERS, crew, groups, block), jnp.float32),
            pltpu.SemaphoreType.DMA((3,)),
            single,
            single,
            single,
            single,
            single,
            single,
            pltpu.SemaphoreType.DMA((3,)),
            single,
            by_group,
            by_group,
            single,
            single,
            pltpu.SemaphoreType.DMA((groups, LAYERS)),
            pltpu.SemaphoreType.DMA((groups, LAYERS)),
            by_layer,
            single,
            by_layer,
            pltpu.SemaphoreType.REGULAR((LAYERS,)),
        ],
        compiler_params=pltpu.CompilerParams(
            collective_id=0, has_side_effects=True, vmem_limit_bytes=VMEM_LIMIT
        ),
    )(inputs, gating, grad_out, filters)
    return pl.pallas_call(
        store_kernel,
        out_shape=outs,
        in_specs=[vmem] * 3,
        out_specs=(hbm, hbm, hbm),
        scratch_shapes=[pltpu.SemaphoreType.DMA((3,))],
        compiler_params=pltpu.CompilerParams(vmem_limit_bytes=1024 * 1024),
    )(*results)


VMEM_LIMIT = 53900 * 1024


def solution(mesh):
    placed = (P("chan", "seq"), P("chan", "seq"), P("chan", "seq"), P(None, ("seq", "chan")))
    layered = mesh.shape["seq"] == 16 and mesh.shape["chan"] == 2
    return jax.shard_map(
        layered_shards if layered else shards,
        mesh=mesh,
        in_specs=placed,
        out_specs=(P("chan", "seq"), P("chan", "seq"), P(None, ("seq", "chan"))),
        check_vma=False,
    )
```

```python
import functools
import math

import jax
import jax.numpy as jnp
from jax import lax
from jax.experimental import pallas as pl
from jax.experimental.pallas import tpu as pltpu
from jax.sharding import PartitionSpec as P

D = 4096
G = 64


HIGHEST = lax.Precision.HIGHEST


def make_tables(seq_count, block_len):
    outer = 2 * seq_count
    total = outer * block_len
    outer_index = jnp.arange(outer, dtype=jnp.int32)
    block_index = jnp.arange(seq_count, dtype=jnp.int32)
    inner_index = jnp.arange(block_len, dtype=jnp.int32)
    block_angle = (outer_index[:, None] * block_index[None, :] % outer).astype(jnp.float32) * (
        2.0 * math.pi / outer
    )
    twist_angle = (outer_index[:, None] * inner_index[None, :] % total).astype(jnp.float32) * (
        2.0 * math.pi / total
    )
    inner_angle = (inner_index[:, None] * inner_index[None, :] % block_len).astype(jnp.float32) * (
        2.0 * math.pi / block_len
    )
    return (
        jnp.cos(block_angle),
        jnp.sin(block_angle),
        jnp.cos(twist_angle),
        jnp.sin(twist_angle),
        jnp.cos(inner_angle),
        jnp.sin(inner_angle),
    )


def right_product(values, table):
    return jnp.einsum("ckm,mj->ckj", values, table, precision=HIGHEST)


def forward_dft(signal, tables):
    block_cos, block_sin, twist_cos, twist_sin, inner_cos, inner_sin = tables
    real_first = jnp.einsum("kn,cnm->ckm", block_cos, signal, precision=HIGHEST)
    imag_first = -jnp.einsum("kn,cnm->ckm", block_sin, signal, precision=HIGHEST)
    real_twist = real_first * twist_cos + imag_first * twist_sin
    imag_twist = imag_first * twist_cos - real_first * twist_sin
    real_spec = right_product(real_twist, inner_cos) + right_product(imag_twist, inner_sin)
    imag_spec = right_product(imag_twist, inner_cos) - right_product(real_twist, inner_sin)
    return (real_spec, imag_spec)


def inverse_dft(real_spec, imag_spec, tables):
    block_cos, block_sin, twist_cos, twist_sin, inner_cos, inner_sin = tables
    real_first = right_product(real_spec, inner_cos) - right_product(imag_spec, inner_sin)
    imag_first = right_product(real_spec, inner_sin) + right_product(imag_spec, inner_cos)
    real_twist = real_first * twist_cos - imag_first * twist_sin
    imag_twist = real_first * twist_sin + imag_first * twist_cos
    total = real_spec.shape[1] * real_spec.shape[2]
    result = jnp.einsum("kn,ckm->cnm", block_cos, real_twist, precision=HIGHEST)
    result = result - jnp.einsum("kn,ckm->cnm", block_sin, imag_twist, precision=HIGHEST)
    return result / total


def shards(inputs, gating, grad_out, filters):
    seq_count = lax.axis_size("seq")
    chan_count = lax.axis_size("chan")
    chan_rows, block_len = inputs.shape
    local_chan = chan_rows // seq_count
    group_width = D // G
    groups_here = G // chan_count
    local_groups = max(1, local_chan // group_width)
    group_share = local_chan // local_groups
    copies = max(1, seq_count // groups_here)
    length = block_len * seq_count
    outer = 2 * seq_count
    factor = 1.0 / math.sqrt(group_width * length)
    tables = make_tables(seq_count, block_len)
    whole = lax.all_gather(filters, ("seq", "chan"), axis=1, tiled=True)
    first_group = (
        lax.axis_index("chan") * chan_rows + lax.axis_index("seq") * local_chan
    ) // group_width
    kernel_rows = lax.dynamic_slice_in_dim(whole, first_group, local_groups, 0)
    kernel_blocks = kernel_rows.reshape(local_groups, seq_count, block_len)
    kernel_real, kernel_imag = forward_dft(kernel_blocks * factor, tables)
    kernel_real = kernel_real[:, None]
    kernel_imag = kernel_imag[:, None]
    shaped_inputs = inputs.reshape(chan_rows, 1, block_len)
    values, gate_part, upstream = (
        lax.all_to_all(shaped_inputs, "seq", split_axis=0, concat_axis=1, tiled=True),
        lax.all_to_all(
            gating.reshape(chan_rows, 1, block_len), "seq", split_axis=0, concat_axis=1, tiled=True
        ),
        lax.all_to_all(
            grad_out.reshape(chan_rows, 1, block_len),
            "seq",
            split_axis=0,
            concat_axis=1,
            tiled=True,
        ),
    )
    input_real, input_imag = forward_dft(values.astype(jnp.float32), tables)
    upstream_f = upstream.astype(jnp.float32)
    product_b = lax.optimization_barrier(
        (gate_part.astype(jnp.float32) * upstream_f).astype(jnp.bfloat16)
    )
    up_real, up_imag = forward_dft(product_b.astype(jnp.float32), tables)
    grouped_shape = (local_groups, group_share, outer, block_len)
    input_real = input_real.reshape(grouped_shape)
    input_imag = input_imag.reshape(grouped_shape)
    up_real = up_real.reshape(grouped_shape)
    up_imag = up_imag.reshape(grouped_shape)
    flat_shape = (local_chan, outer, block_len)
    conv_real = input_real * kernel_real - input_imag * kernel_imag
    conv_imag = input_real * kernel_imag + input_imag * kernel_real
    convolved = inverse_dft(conv_real.reshape(flat_shape), conv_imag.reshape(flat_shape), tables)
    conv_b = convolved.astype(jnp.bfloat16)
    second = (upstream_f * lax.optimization_barrier(conv_b).astype(jnp.float32)).astype(
        jnp.bfloat16
    )
    back_real = up_real * kernel_real + up_imag * kernel_imag
    back_imag = up_imag * kernel_real - up_real * kernel_imag
    grad_input = inverse_dft(
        back_real.reshape(flat_shape), back_imag.reshape(flat_shape), tables
    ).astype(jnp.bfloat16)
    returned_input, returned_second = (
        lax.all_to_all(grad_input, "seq", split_axis=1, concat_axis=0, tiled=True),
        lax.all_to_all(second, "seq", split_axis=1, concat_axis=0, tiled=True),
    )
    returned_second = returned_second.reshape(chan_rows, block_len)
    cross_real = jnp.sum(input_real * up_real + input_imag * up_imag, axis=1)
    cross_imag = jnp.sum(input_real * up_imag - input_imag * up_real, axis=1)
    partial_grad = inverse_dft(cross_real, cross_imag, tables) * factor
    received = lax.all_to_all(partial_grad, "seq", split_axis=1, concat_axis=0, tiled=True)
    summed = received.reshape(groups_here, copies, block_len).sum(axis=1)
    grad_filters = lax.all_to_all(summed, "chan", split_axis=1, concat_axis=0, tiled=True)
    return (returned_input.reshape(chan_rows, block_len), returned_second, grad_filters)


GROUP_WIDTH = D // G
MESH = pl.DeviceIdType.MESH
TILE = 256
LAYERS = 4
LEAD, DELAY_SECOND, DELAY_RELAY, DELAY_COMPUTE, DELAY_OUTER = 4, 1, 2, 3, 6
NT = (((1,), (1,)), ((), ()))
NN = (((1,), (0,)), ((), ()))


def dot(a, b, dims):
    return lax.dot_general(a, b, dims, preferred_element_type=jnp.float32)


def layered_kernel(
    seq_count,
    chan_count,
    x_hbm,
    gate_hbm,
    up_hbm,
    raw_hbm,
    gi_ref,
    gg_ref,
    grad_ref,
    gate_ref,
    up_ref,
    raw_ref,
    filt_ref,
    filt_in,
    filt_layer,
    filt_all,
    u_loc,
    xs,
    us,
    table,
    acc_c,
    acc_g,
    cv,
    gv,
    conv_in,
    far,
    fg_out,
    fg_in,
    load_sem,
    x_send,
    u_send,
    c_send,
    g_send,
    z_send,
    far_send,
    f_send,
    k_send,
    x_recv,
    u_recv,
    c_recv,
    g_recv,
    zx_recv,
    zu_recv,
    f_recv,
    k_recv,
    kz_recv,
    enter_sem,
):
    seq = lax.axis_index("seq")
    chan = lax.axis_index("chan")
    peers = seq_count // LAYERS
    crew = peers * chan_count
    layer = seq // peers
    spot = lax.rem(seq, peers)
    slot = spot * chan_count + chan
    last = LAYERS - 1
    groups = xs.shape[0]
    block = x_hbm.shape[1]
    per_tile = TILE // block
    length = block * seq_count
    tiles = length // TILE
    half = tiles // LAYERS
    width = GROUP_WIDTH
    layer_rows = half * width
    local_chan = groups * width
    share = raw_hbm.shape[1]
    factor = 1.0 / math.sqrt(width * length)

    loads = [
        pltpu.make_async_copy(gate_hbm, gate_ref, load_sem.at[0]),
        pltpu.make_async_copy(up_hbm, up_ref, load_sem.at[1]),
        pltpu.make_async_copy(raw_hbm, raw_ref, load_sem.at[2]),
    ]
    for load in loads:
        load.start()

    barrier = pltpu.get_barrier_semaphore()

    def greet(to_seq, to_chan):
        pl.semaphore_signal(barrier, inc=1, device_id=(to_seq, to_chan), device_id_type=MESH)

    def crew_member(k):
        other = lax.rem(slot + k, crew)
        return other // chan_count, lax.rem(other, chan_count)

    for k in range(1, crew):
        p, c = crew_member(k)
        greet(layer * peers + p, c)
    everyone = [(p, c) for p in range(peers) for c in range(chan_count)]
    lone = [(spot, chan)]
    greeted = {
        0: ((1, everyone), (2, everyone)),
        1: ((0, lone), (2, everyone), (3, everyone)),
        2: ((0, lone), (1, everyone), (3, everyone)),
        3: (),
    }
    for which in range(LAYERS):

        @pl.when(layer == which)
        def _(which=which):
            for to_layer, spots in greeted[which]:
                for p, c in spots:
                    greet(to_layer * peers + p, c)

    fg_out[...] = jnp.zeros_like(fg_out)
    loads[2].wait()
    scaled = raw_ref[...] * factor
    lanes = jnp.concatenate([scaled] * chan_count, axis=1)
    kept = lax.broadcasted_iota(jnp.int32, lanes.shape, 1) // share == chan
    lanes = jnp.where(kept, lanes, 0.0)
    for i in range(crew):
        filt_ref[i] = lanes[i * groups : (i + 1) * groups, :]
    loads[0].wait()
    loads[1].wait()
    u_loc[...] = (
        gate_ref[...].astype(jnp.float32) * up_ref[...].astype(jnp.float32)
    ).astype(jnp.bfloat16)
    expected = {0: 2, 1: 2 * crew, 2: 2 * crew, 3: 2 * crew}
    for which in range(LAYERS):

        @pl.when(layer == which)
        def _(which=which):
            pl.semaphore_wait(barrier, crew - 1 + expected[which])

    def enter(origin, to_layer, p, c):
        pl.semaphore_signal(
            enter_sem.at[origin],
            inc=1,
            device_id=(to_layer * peers + p, c),
            device_id_type=MESH,
        )

    @pl.when(layer == 3)
    def _():
        for p, c in everyone:
            enter(3, 2, p, c)
            enter(3, 1, p, c)

    def place(ref, g, s):
        return ref.at[
            g,
            pl.ds(pl.multiple_of((s // per_tile) * width, width), width),
            pl.ds(pl.multiple_of(lax.rem(s, per_tile) * block, block), block),
        ]

    def strip(ref, q, g):
        return ref.at[pl.ds(pl.multiple_of(q * local_chan + g * width, width), width), :]

    def remote(from_ref, to_ref, send, recv, to_seq, to_chan=None):
        return pltpu.make_async_remote_copy(
            src_ref=from_ref,
            dst_ref=to_ref,
            send_sem=send,
            recv_sem=recv,
            device_id=(to_seq, chan if to_chan is None else to_chan),
            device_id_type=MESH,
        )

    def wait_bytes(ref, sem):
        pltpu.make_async_copy(ref, ref, sem).wait()

    def layer_span(ref, g, which):
        return ref.at[g, pl.ds(pl.multiple_of(which * layer_rows, layer_rows), layer_rows), :]

    def scatter(ref, buf, send, recv, g):
        for k in (2, 3, 1):
            p = lax.rem(spot + k, peers)
            remote(
                strip(ref, p, g), place(buf, g, seq), send.at[0], recv.at[g], layer * peers + p
            ).start()
        pltpu.make_async_copy(strip(ref, spot, g), place(buf, g, seq), recv.at[g]).start()

    def mirror(g):
        return g + 1 - 2 * lax.rem(g, 2)

    def scatter_both(g):
        @pl.when(layer < LAYERS // 2)
        def _():
            scatter(x_hbm, xs, x_send, x_recv, g)
            scatter(u_loc, us, u_send, u_recv, mirror(g))

        @pl.when(layer >= LAYERS // 2)
        def _():
            scatter(u_loc, us, u_send, u_recv, mirror(g))
            scatter(x_hbm, xs, x_send, x_recv, g)

    def give_back(buf, ref, send, recv, g):
        for k in (2, 3, 1):
            p = lax.rem(spot + k, peers)
            remote(
                place(buf, g, p), strip(ref, spot, g), send.at[0], recv.at[0], layer * peers + p
            ).start()
        pltpu.make_async_copy(place(buf, g, spot), strip(ref, spot, g), recv.at[0]).start()

    def send_far(g, ref, recv, to_layer):
        for k in (2, 3, 1, 0):
            p = lax.rem(spot + k, peers)
            remote(
                place(far, g, p), strip(ref, spot, g), far_send.at[0], recv.at[0],
                to_layer * peers + p,
            ).start()

    def hop_x(g, origin, to_layer):
        ref = layer_span(xs, g, origin)
        return remote(ref, ref, z_send.at[0], zx_recv.at[g, origin], to_layer * peers + spot)

    def hop_u(g, origin, to_layer):
        ref = layer_span(us, g, origin)
        return remote(ref, ref, z_send.at[0], zu_recv.at[g, origin], to_layer * peers + spot)

    def ahead(from_ref, buf, recv, origin, to_layer, order=lambda g: g):
        def step(i, carry):
            g = order(i)
            remote(
                strip(from_ref, spot, g), place(buf, g, seq), z_send.at[0], recv.at[g, origin],
                to_layer * peers + spot,
            ).start()
            return carry

        lax.fori_loop(0, groups, step, 0)

    def rest(g, buf, recv, origin, to_layer):
        sibling = spot + 1 - 2 * lax.rem(spot, per_tile)
        tile = origin * half + 1 - spot // per_tile
        refs = (
            place(buf, g, origin * peers + sibling),
            buf.at[g, pl.ds(pl.multiple_of(tile * width, width), width), :],
        )
        for ref in refs:
            remote(
                ref, ref, z_send.at[0], recv.at[g, origin], to_layer * peers + spot
            ).start()

    scatter_both(0)
    for k in range(1, crew):
        p, c = crew_member(k)
        remote(
            filt_ref.at[c * peers + p], filt_in.at[slot], k_send.at[0], k_recv.at[0],
            layer * peers + p, c,
        ).start()
    pltpu.make_async_copy(filt_ref.at[chan * peers + spot], filt_in.at[slot], k_recv.at[0]).start()


    @pl.when(layer == 0)
    def _():
        ahead(x_hbm, xs, zx_recv, 0, 1)

    @pl.when(layer == 1)
    def _():
        ahead(x_hbm, xs, zx_recv, 1, 2)

    @pl.when(layer == 2)
    def _():
        ahead(u_loc, us, zu_recv, 2, 1, mirror)

    @pl.when(layer == 3)
    def _():
        ahead(u_loc, us, zu_recv, 3, 2, mirror)

    def scatter_early(g, carry):
        scatter_both(g)
        return carry

    lax.fori_loop(1, LEAD, scatter_early, 0)

    filt_targets = {0: (1, 2), 1: (2,), 2: (1,), 3: (1, 2)}
    filt_sources = {0: (), 1: (0, 2, 3), 2: (0, 1, 3), 3: (0,)}

    def filt_hop(origin, to_layer):
        return remote(
            filt_layer.at[origin], filt_layer.at[origin], f_send.at[1], kz_recv.at[origin],
            to_layer * peers + spot,
        )

    def spread_filters():
        wait_bytes(filt_in, k_recv.at[0])
        parts = []
        for s in range(peers):
            part = filt_in[s * chan_count]
            for c in range(1, chan_count):
                part = part + filt_in[s * chan_count + c]
            parts.append(part)
        for s in range(peers // 2):
            pair = jnp.concatenate(parts[2 * s : 2 * s + 2], axis=0)
            filt_layer[layer, s] = pair.astype(jnp.bfloat16)
        for which in range(LAYERS):

            @pl.when(layer == which)
            def _(which=which):
                for to in filt_targets[which]:
                    filt_hop(which, to).start()

    def wait_x(g):
        wait_bytes(layer_span(xs, g, layer), x_recv.at[g])

    def wait_u(g):
        wait_bytes(layer_span(us, g, layer), u_recv.at[g])

    def gather_layer(g):
        @pl.when(layer == 0)
        def _():
            wait_x(g)
            rest(g, xs, zx_recv, 0, 1)

        @pl.when(layer == 1)
        def _():
            wait_x(g)
            rest(g, xs, zx_recv, 1, 2)

        @pl.when(layer == 2)
        def _():
            wait_u(mirror(g))
            rest(mirror(g), us, zu_recv, 2, 1)

        @pl.when(layer == 3)
        def _():
            wait_u(mirror(g))
            rest(mirror(g), us, zu_recv, 3, 2)

        @pl.when(g == 0)
        def _():
            spread_filters()

    def second(g):
        @pl.when(layer == 0)
        def _():
            wait_u(mirror(g))
            hop_u(mirror(g), 0, 1).start()

        @pl.when(layer == 3)
        def _():
            wait_x(g)
            hop_x(g, 3, 2).start()

    def relay(g):
        @pl.when(layer == 1)
        def _():
            hop_x(g, 0, 1).wait_recv()
            hop_x(g, 0, 2).start()

        @pl.when(layer == 2)
        def _():
            hop_u(mirror(g), 3, 2).wait_recv()
            hop_u(mirror(g), 3, 1).start()

    row_id = lax.broadcasted_iota(jnp.int32, (TILE, TILE), 0)
    col_id = lax.broadcasted_iota(jnp.int32, (TILE, TILE), 1)
    flip = jnp.where(row_id + col_id == TILE - 1, 1.0, 0.0).astype(jnp.bfloat16)
    row_in = lax.broadcasted_iota(jnp.int32, (block, block), 0)
    col_in = lax.broadcasted_iota(jnp.int32, (block, block), 1)
    upper = col_in >= row_in
    lower_flipped = col_in + row_in >= block - 1

    def compute(g, layers):
        for which in layers:

            @pl.when(layer == which)
            def _(which=which):
                compute_for(which, g)

    def span(first, final):
        return slice(first * width, (final + 1) * width)

    def make_table(g, lags):
        before = jnp.zeros((block, block), jnp.float32)
        for m in range(per_tile * lags):
            row = filt_all[m // peers, m % peers, pl.ds(g, 1), :]
            rolled = pltpu.roll(
                jnp.broadcast_to(row, (block, block)), 0, 1, stride=1, stride_axis=0
            )
            table[m] = jnp.where(upper, rolled, before).astype(jnp.bfloat16)
            before = rolled

    def filter_of(lag):
        rows = []
        for i in range(per_tile):
            parts = []
            for j in range(per_tile):
                m = lag * per_tile + j - i
                parts.append(table[m] if m >= 0 else jnp.zeros((block, block), jnp.bfloat16))
            rows.append(jnp.concatenate(parts, axis=1))
        return jnp.concatenate(rows, axis=0)

    def add(acc, seen, first, final, value):
        runs = []
        for tile in range(first, final + 1):
            if runs and runs[-1][2] == (tile in seen):
                runs[-1][1] = tile
            else:
                runs.append([tile, tile, tile in seen])
        for begin, end, known in runs:
            part = value[(begin - first) * width : (end - first + 1) * width]
            if known:
                acc[span(begin, end), :] += part
            else:
                acc[span(begin, end), :] = part
        seen.update(range(first, final + 1))

    def convolve(g, x_tiles, out_tiles):
        seen = set()
        for lag in range(out_tiles[1] - x_tiles[0] + 1):
            first = max(x_tiles[0], out_tiles[0] - lag)
            final = min(x_tiles[1], out_tiles[1] - lag)
            if first <= final:
                add(
                    acc_c, seen, first + lag, final + lag,
                    dot(xs[g, span(first, final), :], filter_of(lag), NN),
                )

    def correlate(g, u_tiles, out_tiles):
        seen = set()
        for lag in range(u_tiles[1] - out_tiles[0] + 1):
            first = max(u_tiles[0], out_tiles[0] + lag)
            final = min(u_tiles[1], out_tiles[1] + lag)
            if first <= final:
                add(
                    acc_g, seen, first - lag, final - lag,
                    dot(us[g, span(first, final), :], filter_of(lag), NT),
                )

    def filter_grad(g, x_tiles, u_tiles):
        turned = {}

        def turned_from(tile):
            if tile not in turned:
                rows = xs[g, span(tile, x_tiles[1]), :]
                turned[tile] = dot(flip, rows, NT).astype(jnp.bfloat16)
            return turned[tile]

        def gram_of(lag):
            first = max(x_tiles[0], u_tiles[0] - lag)
            final = min(x_tiles[1], u_tiles[1] - lag)
            base = x_tiles[0] + (first - x_tiles[0]) % per_tile
            left = turned_from(base)[:, (first - base) * width : (final + 1 - base) * width]
            return dot(left, us[g, span(first + lag, final + lag), :], NN)

        lags = u_tiles[1] - x_tiles[0] + 1
        zero = jnp.zeros((block, block), jnp.float32)
        gram = gram_of(0)
        current = gram[block:, :block] + gram[:block, block:]
        for lag in range(lags):
            following = gram_of(lag + 1) if lag + 1 < lags else None
            odd = gram[block:, block:]
            if following is None:
                even = zero
            else:
                odd = odd + following[:block, :block]
                even = following[block:, :block] + following[:block, block:]
            for i, (a, b) in enumerate(((current, odd), (odd, even))):
                mixed = jnp.where(lower_flipped, a, b)
                aligned = pltpu.roll(mixed, 1, 1, stride=1, stride_axis=0)
                total = jnp.sum(aligned, axis=0, keepdims=True) * factor
                fg_out[lag * per_tile + i, pl.ds(g, 1), :] = total
            current, gram = even, following

    def send_grads(g, which):
        @pl.when(g == groups - 1)
        def _():
            if which == 1:
                pl.semaphore_wait(enter_sem.at[3], crew)
            for to in range(LAYERS):
                for k in range(1 if to == which else 0, crew):
                    p, c = crew_member(k)
                    remote(
                        fg_out.at[to * peers + p], fg_in.at[which, chan * peers + spot],
                        f_send.at[0], f_recv.at[which], to * peers + p, c,
                    ).start()
            pltpu.make_async_copy(
                fg_out.at[which * peers + spot], fg_in.at[which, chan * peers + spot],
                f_recv.at[which],
            ).start()

    def back_conv(g, tile):
        cv[g] = acc_c[span(tile, tile + half - 1), :].astype(jnp.bfloat16)
        give_back(cv, conv_in, c_send, c_recv, g)

    def back_grad(g, tile):
        gv[g] = acc_g[span(tile, tile + half - 1), :].astype(jnp.bfloat16)
        give_back(gv, gi_ref, g_send, g_recv, g)

    def compute_for(which, g):
        low, high = which * half, (which + 1) * half - 1

        @pl.when(g == 0)
        def _():
            for origin in filt_sources[which]:
                filt_hop(origin, which).wait_recv()
            if which == 2:
                pl.semaphore_wait(enter_sem.at[3], crew)
                filt_hop(0, 3).start()
            for origin in sorted(filt_sources[which] + ((which,) if which < last else ())):
                filt_all[origin] = (
                    filt_layer[origin].astype(jnp.float32).reshape(peers, groups, block)
                )

        other = mirror(g)
        odd = lax.rem(g, 2) == 1
        final = g == groups - 1
        own_step = (jnp.logical_not(odd) & (g > 0)) | final
        if which == 0:
            make_table(g, half)
            convolve(g, (low, high), (low, high))
            back_conv(g, low)
        if which == 1:
            make_table(g, 2 * half)
            convolve(g, (0, high), (low, high))
            back_conv(g, low)
            wait_u(other)
            hop_u(other, 0, 1).wait_recv()

            @pl.when(odd)
            def _():
                filter_grad(g, (0, high), (0, tiles - 1))

            @pl.when(own_step)
            def _():
                filter_grad(g - 2 + g // (groups - 1), (0, high), (0, high))

            send_grads(g, which)
            make_table(other, tiles)
            hop_u(other, 2, 1).wait_recv()
            hop_u(other, 3, 1).wait_recv()
            correlate(other, (0, tiles - 1), (0, high))
            far[other] = acc_g[span(0, low - 1), :].astype(jnp.bfloat16)
            send_far(other, gi_ref, g_recv, 0)
            back_grad(other, low)
        if which == 2:
            make_table(other, 2 * half)
            correlate(other, (low, tiles - 1), (low, high))
            back_grad(other, low)
            wait_x(g)
            hop_x(g, 3, 2).wait_recv()

            @pl.when(odd)
            def _():
                filter_grad(other, (0, tiles - 1), (low, tiles - 1))

            @pl.when(own_step)
            def _():
                filter_grad(g - 1 + g // (groups - 1), (low, tiles - 1), (low, tiles - 1))

            send_grads(g, which)
            make_table(g, tiles)
            hop_x(g, 1, 2).wait_recv()
            hop_x(g, 0, 2).wait_recv()
            convolve(g, (0, tiles - 1), (low, tiles - 1))
            far[g] = acc_c[span(high + 1, tiles - 1), :].astype(jnp.bfloat16)
            send_far(g, conv_in, c_recv, 3)
            back_conv(g, low)
        if which == 3:
            make_table(other, half)
            correlate(other, (low, high), (low, high))
            back_grad(other, low)

    def stage(step, delay, body):
        @pl.when((step >= delay) & (step < groups + delay))
        def _():
            body(step - delay)

    def scatter_later(g):
        @pl.when(g >= LEAD)
        def _():
            scatter_both(g)

    def pipeline(step, carry):
        stage(step, 0, gather_layer)
        stage(step, -LEAD, scatter_later)
        stage(step, DELAY_SECOND, second)
        stage(step, DELAY_RELAY, relay)
        stage(step, DELAY_COMPUTE, lambda g: compute(g, (1, 2)))
        stage(step, DELAY_OUTER, lambda g: compute(g, (0, last)))
        return carry

    lax.fori_loop(0, groups + DELAY_OUTER, pipeline, 0)

    wait_bytes(conv_in, c_recv.at[0])
    gg_ref[...] = (up_ref[...].astype(jnp.float32) * conv_in[...].astype(jnp.float32)).astype(
        jnp.bfloat16
    )
    wait_bytes(gi_ref, g_recv.at[0])
    wait_bytes(fg_in.at[1], f_recv.at[1])
    wait_bytes(fg_in.at[2], f_recv.at[2])
    for i in range(crew):
        total = fg_in[1, i] + fg_in[2, i]
        kept_part = total[:, :share]
        for d in range(1, chan_count):
            kept_part = jnp.where(chan == d, total[:, d * share : (d + 1) * share], kept_part)
        grad_ref[i * groups : (i + 1) * groups, :] = kept_part

    sent = pl.ds(0, groups * (peers - 1) // peers)
    wait_bytes(cv.at[sent], x_send.at[0])
    wait_bytes(cv.at[sent], u_send.at[0])
    wait_bytes(filt_in.at[pl.ds(0, crew - 1)], k_send.at[0])
    wait_bytes(cv, z_send.at[0])
    wait_bytes(cv, z_send.at[0])
    for which in range(LAYERS):

        @pl.when(layer == which)
        def _(which=which):
            if which < last:
                wait_bytes(cv.at[sent], c_send.at[0])
            if which > 0:
                wait_bytes(cv.at[sent], g_send.at[0])
            if which in (1, 2):
                wait_bytes(cv, far_send.at[0])
            for _ in filt_targets[which] + ((3,) if which == 2 else ()):
                wait_bytes(filt_layer.at[0], f_send.at[1])
            if which in (1, 2):
                for _ in range(LAYERS - 1):
                    wait_bytes(fg_in.at[0], f_send.at[0])
                wait_bytes(fg_in.at[0, pl.ds(0, crew - 1)], f_send.at[0])


def store_kernel(a_ref, b_ref, c_ref, a_out, b_out, c_out, sems):
    copies = [
        pltpu.make_async_copy(a_ref, a_out, sems.at[0]),
        pltpu.make_async_copy(b_ref, b_out, sems.at[1]),
        pltpu.make_async_copy(c_ref, c_out, sems.at[2]),
    ]
    for copy in copies:
        copy.start()
    for copy in copies:
        copy.wait()


def layered_shards(inputs, gating, grad_out, filters):
    seq_count = lax.axis_size("seq")
    chan_count = lax.axis_size("chan")
    chan_rows, block = inputs.shape
    peers = seq_count // LAYERS
    crew = peers * chan_count
    groups = chan_rows // peers // GROUP_WIDTH
    length = block * seq_count
    tiles = length // TILE
    rows = tiles * GROUP_WIDTH
    layer_rows = rows // LAYERS
    blocks = length // block
    vmem = pl.BlockSpec(memory_space=pltpu.VMEM)
    hbm = pl.BlockSpec(memory_space=pltpu.HBM)
    single = pltpu.SemaphoreType.DMA((1,))
    by_group = pltpu.SemaphoreType.DMA((groups,))
    by_layer = pltpu.SemaphoreType.DMA((LAYERS,))
    flat = pltpu.VMEM((chan_rows, block), jnp.bfloat16)
    layered = pltpu.VMEM((groups, layer_rows, TILE), jnp.bfloat16)
    small = pltpu.VMEM((crew, groups, block), jnp.float32)
    outs = (
        jax.ShapeDtypeStruct((chan_rows, block), jnp.bfloat16),
        jax.ShapeDtypeStruct((chan_rows, block), jnp.bfloat16),
        jax.ShapeDtypeStruct(filters.shape, jnp.float32),
    )
    results = pl.pallas_call(
        functools.partial(layered_kernel, seq_count, chan_count),
        out_shape=outs,
        in_specs=[hbm] * 4,
        out_specs=(vmem, vmem, vmem),
        scratch_shapes=[
            flat,
            flat,
            pltpu.VMEM(filters.shape, jnp.float32),
            small,
            small,
            pltpu.VMEM((LAYERS, peers // 2, 2 * groups, block), jnp.bfloat16),
            pltpu.VMEM((LAYERS, peers, groups, block), jnp.float32),
            flat,
            pltpu.VMEM((groups, rows, TILE), jnp.bfloat16),
            pltpu.VMEM((groups, rows, TILE), jnp.bfloat16),
            pltpu.VMEM((blocks, block, block), jnp.bfloat16),
            pltpu.VMEM((rows, TILE), jnp.float32),
            pltpu.VMEM((rows, TILE), jnp.float32),
            layered,
            layered,
            flat,
            layered,
            pltpu.VMEM((blocks, groups, block), jnp.float32),
            pltpu.VMEM((LAYERS, crew, groups, block), jnp.float32),
            pltpu.SemaphoreType.DMA((3,)),
            single,
            single,
            single,
            single,
            single,
            single,
            pltpu.SemaphoreType.DMA((3,)),
            single,
            by_group,
            by_group,
            single,
            single,
            pltpu.SemaphoreType.DMA((groups, LAYERS)),
            pltpu.SemaphoreType.DMA((groups, LAYERS)),
            by_layer,
            single,
            by_layer,
            pltpu.SemaphoreType.REGULAR((LAYERS,)),
        ],
        compiler_params=pltpu.CompilerParams(
            collective_id=0, has_side_effects=True, vmem_limit_bytes=VMEM_LIMIT
        ),
    )(inputs, gating, grad_out, filters)
    return pl.pallas_call(
        store_kernel,
        out_shape=outs,
        in_specs=[vmem] * 3,
        out_specs=(hbm, hbm, hbm),
        scratch_shapes=[pltpu.SemaphoreType.DMA((3,))],
        compiler_params=pltpu.CompilerParams(vmem_limit_bytes=1024 * 1024),
    )(*results)


VMEM_LIMIT = 53900 * 1024


def solution(mesh):
    placed = (P("chan", "seq"), P("chan", "seq"), P("chan", "seq"), P(None, ("seq", "chan")))
    layered = mesh.shape["seq"] == 16 and mesh.shape["chan"] == 2
    return jax.shard_map(
        layered_shards if layered else shards,
        mesh=mesh,
        in_specs=placed,
        out_specs=(P("chan", "seq"), P("chan", "seq"), P(None, ("seq", "chan"))),
        check_vma=False,
    )
```

```python
import functools
import math

import jax
import jax.numpy as jnp
from jax import lax
from jax.experimental import pallas as pl
from jax.experimental.pallas import tpu as pltpu
from jax.sharding import PartitionSpec as P

D = 4096
G = 64


HIGHEST = lax.Precision.HIGHEST


def make_tables(seq_count, block_len):
    outer = 2 * seq_count
    total = outer * block_len
    outer_index = jnp.arange(outer, dtype=jnp.int32)
    block_index = jnp.arange(seq_count, dtype=jnp.int32)
    inner_index = jnp.arange(block_len, dtype=jnp.int32)
    block_angle = (outer_index[:, None] * block_index[None, :] % outer).astype(jnp.float32) * (
        2.0 * math.pi / outer
    )
    twist_angle = (outer_index[:, None] * inner_index[None, :] % total).astype(jnp.float32) * (
        2.0 * math.pi / total
    )
    inner_angle = (inner_index[:, None] * inner_index[None, :] % block_len).astype(jnp.float32) * (
        2.0 * math.pi / block_len
    )
    return (
        jnp.cos(block_angle),
        jnp.sin(block_angle),
        jnp.cos(twist_angle),
        jnp.sin(twist_angle),
        jnp.cos(inner_angle),
        jnp.sin(inner_angle),
    )


def right_product(values, table):
    return jnp.einsum("ckm,mj->ckj", values, table, precision=HIGHEST)


def forward_dft(signal, tables):
    block_cos, block_sin, twist_cos, twist_sin, inner_cos, inner_sin = tables
    real_first = jnp.einsum("kn,cnm->ckm", block_cos, signal, precision=HIGHEST)
    imag_first = -jnp.einsum("kn,cnm->ckm", block_sin, signal, precision=HIGHEST)
    real_twist = real_first * twist_cos + imag_first * twist_sin
    imag_twist = imag_first * twist_cos - real_first * twist_sin
    real_spec = right_product(real_twist, inner_cos) + right_product(imag_twist, inner_sin)
    imag_spec = right_product(imag_twist, inner_cos) - right_product(real_twist, inner_sin)
    return (real_spec, imag_spec)


def inverse_dft(real_spec, imag_spec, tables):
    block_cos, block_sin, twist_cos, twist_sin, inner_cos, inner_sin = tables
    real_first = right_product(real_spec, inner_cos) - right_product(imag_spec, inner_sin)
    imag_first = right_product(real_spec, inner_sin) + right_product(imag_spec, inner_cos)
    real_twist = real_first * twist_cos - imag_first * twist_sin
    imag_twist = real_first * twist_sin + imag_first * twist_cos
    total = real_spec.shape[1] * real_spec.shape[2]
    result = jnp.einsum("kn,ckm->cnm", block_cos, real_twist, precision=HIGHEST)
    result = result - jnp.einsum("kn,ckm->cnm", block_sin, imag_twist, precision=HIGHEST)
    return result / total


def shards(inputs, gating, grad_out, filters):
    seq_count = lax.axis_size("seq")
    chan_count = lax.axis_size("chan")
    chan_rows, block_len = inputs.shape
    local_chan = chan_rows // seq_count
    group_width = D // G
    groups_here = G // chan_count
    local_groups = max(1, local_chan // group_width)
    group_share = local_chan // local_groups
    copies = max(1, seq_count // groups_here)
    length = block_len * seq_count
    outer = 2 * seq_count
    factor = 1.0 / math.sqrt(group_width * length)
    tables = make_tables(seq_count, block_len)
    whole = lax.all_gather(filters, ("seq", "chan"), axis=1, tiled=True)
    first_group = (
        lax.axis_index("chan") * chan_rows + lax.axis_index("seq") * local_chan
    ) // group_width
    kernel_rows = lax.dynamic_slice_in_dim(whole, first_group, local_groups, 0)
    kernel_blocks = kernel_rows.reshape(local_groups, seq_count, block_len)
    kernel_real, kernel_imag = forward_dft(kernel_blocks * factor, tables)
    kernel_real = kernel_real[:, None]
    kernel_imag = kernel_imag[:, None]
    shaped_inputs = inputs.reshape(chan_rows, 1, block_len)
    values, gate_part, upstream = (
        lax.all_to_all(shaped_inputs, "seq", split_axis=0, concat_axis=1, tiled=True),
        lax.all_to_all(
            gating.reshape(chan_rows, 1, block_len), "seq", split_axis=0, concat_axis=1, tiled=True
        ),
        lax.all_to_all(
            grad_out.reshape(chan_rows, 1, block_len),
            "seq",
            split_axis=0,
            concat_axis=1,
            tiled=True,
        ),
    )
    input_real, input_imag = forward_dft(values.astype(jnp.float32), tables)
    upstream_f = upstream.astype(jnp.float32)
    product_b = lax.optimization_barrier(
        (gate_part.astype(jnp.float32) * upstream_f).astype(jnp.bfloat16)
    )
    up_real, up_imag = forward_dft(product_b.astype(jnp.float32), tables)
    grouped_shape = (local_groups, group_share, outer, block_len)
    input_real = input_real.reshape(grouped_shape)
    input_imag = input_imag.reshape(grouped_shape)
    up_real = up_real.reshape(grouped_shape)
    up_imag = up_imag.reshape(grouped_shape)
    flat_shape = (local_chan, outer, block_len)
    conv_real = input_real * kernel_real - input_imag * kernel_imag
    conv_imag = input_real * kernel_imag + input_imag * kernel_real
    convolved = inverse_dft(conv_real.reshape(flat_shape), conv_imag.reshape(flat_shape), tables)
    conv_b = convolved.astype(jnp.bfloat16)
    second = (upstream_f * lax.optimization_barrier(conv_b).astype(jnp.float32)).astype(
        jnp.bfloat16
    )
    back_real = up_real * kernel_real + up_imag * kernel_imag
    back_imag = up_imag * kernel_real - up_real * kernel_imag
    grad_input = inverse_dft(
        back_real.reshape(flat_shape), back_imag.reshape(flat_shape), tables
    ).astype(jnp.bfloat16)
    returned_input, returned_second = (
        lax.all_to_all(grad_input, "seq", split_axis=1, concat_axis=0, tiled=True),
        lax.all_to_all(second, "seq", split_axis=1, concat_axis=0, tiled=True),
    )
    returned_second = returned_second.reshape(chan_rows, block_len)
    cross_real = jnp.sum(input_real * up_real + input_imag * up_imag, axis=1)
    cross_imag = jnp.sum(input_real * up_imag - input_imag * up_real, axis=1)
    partial_grad = inverse_dft(cross_real, cross_imag, tables) * factor
    received = lax.all_to_all(partial_grad, "seq", split_axis=1, concat_axis=0, tiled=True)
    summed = received.reshape(groups_here, copies, block_len).sum(axis=1)
    grad_filters = lax.all_to_all(summed, "chan", split_axis=1, concat_axis=0, tiled=True)
    return (returned_input.reshape(chan_rows, block_len), returned_second, grad_filters)


GROUP_WIDTH = D // G
MESH = pl.DeviceIdType.MESH
TILE = 256
LAYERS = 4
LEAD, DELAY_SECOND, DELAY_RELAY, DELAY_COMPUTE, DELAY_OUTER = 6, 1, 2, 3, 6
NT = (((1,), (1,)), ((), ()))
NN = (((1,), (0,)), ((), ()))


def dot(a, b, dims):
    return lax.dot_general(a, b, dims, preferred_element_type=jnp.float32)


def layered_kernel(
    seq_count,
    chan_count,
    x_hbm,
    gate_hbm,
    up_hbm,
    raw_hbm,
    gi_ref,
    gg_ref,
    grad_ref,
    gate_ref,
    up_ref,
    raw_ref,
    filt_ref,
    filt_in,
    filt_layer,
    filt_all,
    u_loc,
    xs,
    us,
    table,
    acc_c,
    acc_g,
    cv,
    gv,
    conv_in,
    far,
    fg_out,
    fg_in,
    load_sem,
    x_send,
    u_send,
    c_send,
    g_send,
    z_send,
    far_send,
    f_send,
    k_send,
    x_recv,
    u_recv,
    c_recv,
    g_recv,
    zx_recv,
    zu_recv,
    f_recv,
    k_recv,
    kz_recv,
    enter_sem,
):
    seq = lax.axis_index("seq")
    chan = lax.axis_index("chan")
    peers = seq_count // LAYERS
    crew = peers * chan_count
    layer = seq // peers
    spot = lax.rem(seq, peers)
    slot = spot * chan_count + chan
    last = LAYERS - 1
    groups = xs.shape[0]
    block = x_hbm.shape[1]
    per_tile = TILE // block
    length = block * seq_count
    tiles = length // TILE
    half = tiles // LAYERS
    width = GROUP_WIDTH
    layer_rows = half * width
    local_chan = groups * width
    share = raw_hbm.shape[1]
    factor = 1.0 / math.sqrt(width * length)

    loads = [
        pltpu.make_async_copy(gate_hbm, gate_ref, load_sem.at[0]),
        pltpu.make_async_copy(up_hbm, up_ref, load_sem.at[1]),
        pltpu.make_async_copy(raw_hbm, raw_ref, load_sem.at[2]),
    ]
    for load in loads:
        load.start()

    barrier = pltpu.get_barrier_semaphore()

    def greet(to_seq, to_chan):
        pl.semaphore_signal(barrier, inc=1, device_id=(to_seq, to_chan), device_id_type=MESH)

    def crew_member(k):
        other = lax.rem(slot + k, crew)
        return other // chan_count, lax.rem(other, chan_count)

    for k in range(1, crew):
        p, c = crew_member(k)
        greet(layer * peers + p, c)
    everyone = [(p, c) for p in range(peers) for c in range(chan_count)]
    lone = [(spot, chan)]
    greeted = {
        0: ((1, everyone), (2, everyone)),
        1: ((0, lone), (2, everyone), (3, everyone)),
        2: ((0, lone), (1, everyone), (3, everyone)),
        3: (),
    }
    for which in range(LAYERS):

        @pl.when(layer == which)
        def _(which=which):
            for to_layer, spots in greeted[which]:
                for p, c in spots:
                    greet(to_layer * peers + p, c)

    fg_out[...] = jnp.zeros_like(fg_out)
    loads[2].wait()
    scaled = raw_ref[...] * factor
    lanes = jnp.concatenate([scaled] * chan_count, axis=1)
    kept = lax.broadcasted_iota(jnp.int32, lanes.shape, 1) // share == chan
    lanes = jnp.where(kept, lanes, 0.0)
    for i in range(crew):
        filt_ref[i] = lanes[i * groups : (i + 1) * groups, :]
    loads[0].wait()
    loads[1].wait()
    u_loc[...] = (
        gate_ref[...].astype(jnp.float32) * up_ref[...].astype(jnp.float32)
    ).astype(jnp.bfloat16)
    expected = {0: 2, 1: 2 * crew, 2: 2 * crew, 3: 2 * crew}
    for which in range(LAYERS):

        @pl.when(layer == which)
        def _(which=which):
            pl.semaphore_wait(barrier, crew - 1 + expected[which])

    def enter(origin, to_layer, p, c):
        pl.semaphore_signal(
            enter_sem.at[origin],
            inc=1,
            device_id=(to_layer * peers + p, c),
            device_id_type=MESH,
        )

    @pl.when(layer == 3)
    def _():
        for p, c in everyone:
            enter(3, 2, p, c)
            enter(3, 1, p, c)

    def place(ref, g, s):
        return ref.at[
            g,
            pl.ds(pl.multiple_of((s // per_tile) * width, width), width),
            pl.ds(pl.multiple_of(lax.rem(s, per_tile) * block, block), block),
        ]

    def strip(ref, q, g):
        return ref.at[pl.ds(pl.multiple_of(q * local_chan + g * width, width), width), :]

    def remote(from_ref, to_ref, send, recv, to_seq, to_chan=None):
        return pltpu.make_async_remote_copy(
            src_ref=from_ref,
            dst_ref=to_ref,
            send_sem=send,
            recv_sem=recv,
            device_id=(to_seq, chan if to_chan is None else to_chan),
            device_id_type=MESH,
        )

    def wait_bytes(ref, sem):
        pltpu.make_async_copy(ref, ref, sem).wait()

    def layer_span(ref, g, which):
        return ref.at[g, pl.ds(pl.multiple_of(which * layer_rows, layer_rows), layer_rows), :]

    def scatter(ref, buf, send, recv, g):
        for k in (2, 3, 1):
            p = lax.rem(spot + k, peers)
            remote(
                strip(ref, p, g), place(buf, g, seq), send.at[0], recv.at[g], layer * peers + p
            ).start()
        pltpu.make_async_copy(strip(ref, spot, g), place(buf, g, seq), recv.at[g]).start()

    def mirror(g):
        return g + 1 - 2 * lax.rem(g, 2)

    def scatter_both(g):
        @pl.when(layer < LAYERS // 2)
        def _():
            scatter(x_hbm, xs, x_send, x_recv, g)
            scatter(u_loc, us, u_send, u_recv, mirror(g))

        @pl.when(layer >= LAYERS // 2)
        def _():
            scatter(u_loc, us, u_send, u_recv, mirror(g))
            scatter(x_hbm, xs, x_send, x_recv, g)

    def give_back(buf, ref, send, recv, g):
        for k in (2, 3, 1):
            p = lax.rem(spot + k, peers)
            remote(
                place(buf, g, p), strip(ref, spot, g), send.at[0], recv.at[0], layer * peers + p
            ).start()
        pltpu.make_async_copy(place(buf, g, spot), strip(ref, spot, g), recv.at[0]).start()

    def send_far(g, ref, recv, to_layer):
        for p in range(peers):
            remote(
                place(far, g, p), strip(ref, spot, g), far_send.at[0], recv.at[0],
                to_layer * peers + p,
            ).start()

    def hop_x(g, origin, to_layer):
        ref = layer_span(xs, g, origin)
        return remote(ref, ref, z_send.at[0], zx_recv.at[g, origin], to_layer * peers + spot)

    def hop_u(g, origin, to_layer):
        ref = layer_span(us, g, origin)
        return remote(ref, ref, z_send.at[0], zu_recv.at[g, origin], to_layer * peers + spot)

    def ahead(from_ref, buf, recv, origin, to_layer, order=lambda g: g):
        def step(i, carry):
            g = order(i)
            remote(
                strip(from_ref, spot, g), place(buf, g, seq), z_send.at[0], recv.at[g, origin],
                to_layer * peers + spot,
            ).start()
            return carry

        lax.fori_loop(0, groups, step, 0)

    def rest(g, buf, recv, origin, to_layer):
        sibling = spot + 1 - 2 * lax.rem(spot, per_tile)
        tile = origin * half + 1 - spot // per_tile
        refs = (
            place(buf, g, origin * peers + sibling),
            buf.at[g, pl.ds(pl.multiple_of(tile * width, width), width), :],
        )
        for ref in refs:
            remote(
                ref, ref, z_send.at[0], recv.at[g, origin], to_layer * peers + spot
            ).start()

    scatter_both(0)

    @pl.when(layer == 0)
    def _():
        ahead(x_hbm, xs, zx_recv, 0, 1)

    @pl.when(layer == 1)
    def _():
        ahead(x_hbm, xs, zx_recv, 1, 2)

    @pl.when(layer == 2)
    def _():
        ahead(u_loc, us, zu_recv, 2, 1, mirror)

    @pl.when(layer == 3)
    def _():
        ahead(u_loc, us, zu_recv, 3, 2, mirror)

    for k in range(1, crew):
        p, c = crew_member(k)
        remote(
            filt_ref.at[c * peers + p], filt_in.at[slot], k_send.at[0], k_recv.at[0],
            layer * peers + p, c,
        ).start()
    pltpu.make_async_copy(filt_ref.at[chan * peers + spot], filt_in.at[slot], k_recv.at[0]).start()

    def scatter_early(g, carry):
        scatter_both(g)
        return carry

    lax.fori_loop(1, LEAD, scatter_early, 0)

    filt_targets = {0: (1, 2), 1: (2,), 2: (1,), 3: (1, 2)}
    filt_sources = {0: (), 1: (0, 2, 3), 2: (0, 1, 3), 3: (0,)}

    def filt_hop(origin, to_layer):
        return remote(
            filt_layer.at[origin], filt_layer.at[origin], f_send.at[1], kz_recv.at[origin],
            to_layer * peers + spot,
        )

    def spread_filters():
        wait_bytes(filt_in, k_recv.at[0])
        parts = []
        for s in range(peers):
            part = filt_in[s * chan_count]
            for c in range(1, chan_count):
                part = part + filt_in[s * chan_count + c]
            parts.append(part)
        for s in range(peers // 2):
            pair = jnp.concatenate(parts[2 * s : 2 * s + 2], axis=0)
            filt_layer[layer, s] = pair.astype(jnp.bfloat16)
        for which in range(LAYERS):

            @pl.when(layer == which)
            def _(which=which):
                for to in filt_targets[which]:
                    filt_hop(which, to).start()

    def wait_x(g):
        wait_bytes(layer_span(xs, g, layer), x_recv.at[g])

    def wait_u(g):
        wait_bytes(layer_span(us, g, layer), u_recv.at[g])

    def gather_layer(g):
        @pl.when(layer == 0)
        def _():
            wait_x(g)
            rest(g, xs, zx_recv, 0, 1)

        @pl.when(layer == 1)
        def _():
            wait_x(g)
            rest(g, xs, zx_recv, 1, 2)

        @pl.when(layer == 2)
        def _():
            wait_u(mirror(g))
            rest(mirror(g), us, zu_recv, 2, 1)

        @pl.when(layer == 3)
        def _():
            wait_u(mirror(g))
            rest(mirror(g), us, zu_recv, 3, 2)

        @pl.when(g == 0)
        def _():
            spread_filters()

    def second(g):
        @pl.when(layer == 0)
        def _():
            wait_u(mirror(g))
            hop_u(mirror(g), 0, 1).start()

        @pl.when(layer == 3)
        def _():
            wait_x(g)
            hop_x(g, 3, 2).start()

    def relay(g):
        @pl.when(layer == 1)
        def _():
            hop_x(g, 0, 1).wait_recv()
            hop_x(g, 0, 2).start()

        @pl.when(layer == 2)
        def _():
            hop_u(mirror(g), 3, 2).wait_recv()
            hop_u(mirror(g), 3, 1).start()

    row_id = lax.broadcasted_iota(jnp.int32, (TILE, TILE), 0)
    col_id = lax.broadcasted_iota(jnp.int32, (TILE, TILE), 1)
    flip = jnp.where(row_id + col_id == TILE - 1, 1.0, 0.0).astype(jnp.bfloat16)
    row_in = lax.broadcasted_iota(jnp.int32, (block, block), 0)
    col_in = lax.broadcasted_iota(jnp.int32, (block, block), 1)
    upper = col_in >= row_in
    lower_flipped = col_in + row_in >= block - 1

    def compute(g, layers):
        for which in layers:

            @pl.when(layer == which)
            def _(which=which):
                compute_for(which, g)

    def span(first, final):
        return slice(first * width, (final + 1) * width)

    def make_table(g, lags):
        before = jnp.zeros((block, block), jnp.float32)
        for m in range(per_tile * lags):
            row = filt_all[m // peers, m % peers, pl.ds(g, 1), :]
            rolled = pltpu.roll(
                jnp.broadcast_to(row, (block, block)), 0, 1, stride=1, stride_axis=0
            )
            table[m] = jnp.where(upper, rolled, before).astype(jnp.bfloat16)
            before = rolled

    def filter_of(lag):
        rows = []
        for i in range(per_tile):
            parts = []
            for j in range(per_tile):
                m = lag * per_tile + j - i
                parts.append(table[m] if m >= 0 else jnp.zeros((block, block), jnp.bfloat16))
            rows.append(jnp.concatenate(parts, axis=1))
        return jnp.concatenate(rows, axis=0)

    def add(acc, seen, first, final, value):
        runs = []
        for tile in range(first, final + 1):
            if runs and runs[-1][2] == (tile in seen):
                runs[-1][1] = tile
            else:
                runs.append([tile, tile, tile in seen])
        for begin, end, known in runs:
            part = value[(begin - first) * width : (end - first + 1) * width]
            if known:
                acc[span(begin, end), :] += part
            else:
                acc[span(begin, end), :] = part
        seen.update(range(first, final + 1))

    def convolve(g, x_tiles, out_tiles):
        seen = set()
        for lag in range(out_tiles[1] - x_tiles[0] + 1):
            first = max(x_tiles[0], out_tiles[0] - lag)
            final = min(x_tiles[1], out_tiles[1] - lag)
            if first <= final:
                add(
                    acc_c, seen, first + lag, final + lag,
                    dot(xs[g, span(first, final), :], filter_of(lag), NN),
                )

    def correlate(g, u_tiles, out_tiles):
        seen = set()
        for lag in range(u_tiles[1] - out_tiles[0] + 1):
            first = max(u_tiles[0], out_tiles[0] + lag)
            final = min(u_tiles[1], out_tiles[1] + lag)
            if first <= final:
                add(
                    acc_g, seen, first - lag, final - lag,
                    dot(us[g, span(first, final), :], filter_of(lag), NT),
                )

    def filter_grad(g, x_tiles, u_tiles):
        turned = {}

        def turned_from(tile):
            if tile not in turned:
                rows = xs[g, span(tile, x_tiles[1]), :]
                turned[tile] = dot(flip, rows, NT).astype(jnp.bfloat16)
            return turned[tile]

        def gram_of(lag):
            first = max(x_tiles[0], u_tiles[0] - lag)
            final = min(x_tiles[1], u_tiles[1] - lag)
            base = x_tiles[0] + (first - x_tiles[0]) % per_tile
            left = turned_from(base)[:, (first - base) * width : (final + 1 - base) * width]
            return dot(left, us[g, span(first + lag, final + lag), :], NN)

        lags = u_tiles[1] - x_tiles[0] + 1
        zero = jnp.zeros((block, block), jnp.float32)
        gram = gram_of(0)
        current = gram[block:, :block] + gram[:block, block:]
        for lag in range(lags):
            following = gram_of(lag + 1) if lag + 1 < lags else None
            odd = gram[block:, block:]
            if following is None:
                even = zero
            else:
                odd = odd + following[:block, :block]
                even = following[block:, :block] + following[:block, block:]
            for i, (a, b) in enumerate(((current, odd), (odd, even))):
                mixed = jnp.where(lower_flipped, a, b)
                aligned = pltpu.roll(mixed, 1, 1, stride=1, stride_axis=0)
                total = jnp.sum(aligned, axis=0, keepdims=True) * factor
                fg_out[lag * per_tile + i, pl.ds(g, 1), :] = total
            current, gram = even, following

    def send_grads(g, which):
        @pl.when(g == groups - 1)
        def _():
            if which == 1:
                pl.semaphore_wait(enter_sem.at[3], crew)
            for to in range(LAYERS):
                for k in range(1 if to == which else 0, crew):
                    p, c = crew_member(k)
                    remote(
                        fg_out.at[to * peers + p], fg_in.at[which, chan * peers + spot],
                        f_send.at[0], f_recv.at[which], to * peers + p, c,
                    ).start()
            pltpu.make_async_copy(
                fg_out.at[which * peers + spot], fg_in.at[which, chan * peers + spot],
                f_recv.at[which],
            ).start()

    def back_conv(g, tile):
        cv[g] = acc_c[span(tile, tile + half - 1), :].astype(jnp.bfloat16)
        give_back(cv, conv_in, c_send, c_recv, g)

    def back_grad(g, tile):
        gv[g] = acc_g[span(tile, tile + half - 1), :].astype(jnp.bfloat16)
        give_back(gv, gi_ref, g_send, g_recv, g)

    def compute_for(which, g):
        low, high = which * half, (which + 1) * half - 1

        @pl.when(g == 0)
        def _():
            for origin in filt_sources[which]:
                filt_hop(origin, which).wait_recv()
            if which == 2:
                pl.semaphore_wait(enter_sem.at[3], crew)
                filt_hop(0, 3).start()
            for origin in sorted(filt_sources[which] + ((which,) if which < last else ())):
                filt_all[origin] = (
                    filt_layer[origin].astype(jnp.float32).reshape(peers, groups, block)
                )

        other = mirror(g)
        odd = lax.rem(g, 2) == 1
        final = g == groups - 1
        own_step = (jnp.logical_not(odd) & (g > 0)) | final
        if which == 0:
            make_table(g, half)
            convolve(g, (low, high), (low, high))
            back_conv(g, low)
        if which == 1:
            make_table(g, 2 * half)
            convolve(g, (0, high), (low, high))
            back_conv(g, low)
            wait_u(other)
            hop_u(other, 0, 1).wait_recv()

            @pl.when(odd)
            def _():
                filter_grad(g, (0, high), (0, tiles - 1))

            @pl.when(own_step)
            def _():
                filter_grad(g - 2 + g // (groups - 1), (0, high), (0, high))

            send_grads(g, which)
            make_table(other, tiles)
            hop_u(other, 2, 1).wait_recv()
            hop_u(other, 3, 1).wait_recv()
            correlate(other, (0, tiles - 1), (0, high))
            far[other] = acc_g[span(0, low - 1), :].astype(jnp.bfloat16)
            send_far(other, gi_ref, g_recv, 0)
            back_grad(other, low)
        if which == 2:
            make_table(other, 2 * half)
            correlate(other, (low, tiles - 1), (low, high))
            back_grad(other, low)
            wait_x(g)
            hop_x(g, 3, 2).wait_recv()

            @pl.when(odd)
            def _():
                filter_grad(other, (0, tiles - 1), (low, tiles - 1))

            @pl.when(own_step)
            def _():
                filter_grad(g - 1 + g // (groups - 1), (low, tiles - 1), (low, tiles - 1))

            send_grads(g, which)
            make_table(g, tiles)
            hop_x(g, 1, 2).wait_recv()
            hop_x(g, 0, 2).wait_recv()
            convolve(g, (0, tiles - 1), (low, tiles - 1))
            far[g] = acc_c[span(high + 1, tiles - 1), :].astype(jnp.bfloat16)
            send_far(g, conv_in, c_recv, 3)
            back_conv(g, low)
        if which == 3:
            make_table(other, half)
            correlate(other, (low, high), (low, high))
            back_grad(other, low)

    def stage(step, delay, body):
        @pl.when((step >= delay) & (step < groups + delay))
        def _():
            body(step - delay)

    def scatter_later(g):
        @pl.when(g >= LEAD)
        def _():
            scatter_both(g)

    def pipeline(step, carry):
        stage(step, 0, gather_layer)
        stage(step, -LEAD, scatter_later)
        stage(step, DELAY_SECOND, second)
        stage(step, DELAY_RELAY, relay)
        stage(step, DELAY_COMPUTE, lambda g: compute(g, (1, 2)))
        stage(step, DELAY_OUTER, lambda g: compute(g, (0, last)))
        return carry

    lax.fori_loop(0, groups + DELAY_OUTER, pipeline, 0)

    wait_bytes(conv_in, c_recv.at[0])
    gg_ref[...] = (up_ref[...].astype(jnp.float32) * conv_in[...].astype(jnp.float32)).astype(
        jnp.bfloat16
    )
    wait_bytes(gi_ref, g_recv.at[0])
    wait_bytes(fg_in.at[1], f_recv.at[1])
    wait_bytes(fg_in.at[2], f_recv.at[2])
    for i in range(crew):
        total = fg_in[1, i] + fg_in[2, i]
        kept_part = total[:, :share]
        for d in range(1, chan_count):
            kept_part = jnp.where(chan == d, total[:, d * share : (d + 1) * share], kept_part)
        grad_ref[i * groups : (i + 1) * groups, :] = kept_part

    sent = pl.ds(0, groups * (peers - 1) // peers)
    wait_bytes(cv.at[sent], x_send.at[0])
    wait_bytes(cv.at[sent], u_send.at[0])
    wait_bytes(filt_in.at[pl.ds(0, crew - 1)], k_send.at[0])
    wait_bytes(cv, z_send.at[0])
    wait_bytes(cv, z_send.at[0])
    for which in range(LAYERS):

        @pl.when(layer == which)
        def _(which=which):
            if which < last:
                wait_bytes(cv.at[sent], c_send.at[0])
            if which > 0:
                wait_bytes(cv.at[sent], g_send.at[0])
            if which in (1, 2):
                wait_bytes(cv, far_send.at[0])
            for _ in filt_targets[which] + ((3,) if which == 2 else ()):
                wait_bytes(filt_layer.at[0], f_send.at[1])
            if which in (1, 2):
                for _ in range(LAYERS - 1):
                    wait_bytes(fg_in.at[0], f_send.at[0])
                wait_bytes(fg_in.at[0, pl.ds(0, crew - 1)], f_send.at[0])


def store_kernel(a_ref, b_ref, c_ref, a_out, b_out, c_out, sems):
    copies = [
        pltpu.make_async_copy(a_ref, a_out, sems.at[0]),
        pltpu.make_async_copy(b_ref, b_out, sems.at[1]),
        pltpu.make_async_copy(c_ref, c_out, sems.at[2]),
    ]
    for copy in copies:
        copy.start()
    for copy in copies:
        copy.wait()


def layered_shards(inputs, gating, grad_out, filters):
    seq_count = lax.axis_size("seq")
    chan_count = lax.axis_size("chan")
    chan_rows, block = inputs.shape
    peers = seq_count // LAYERS
    crew = peers * chan_count
    groups = chan_rows // peers // GROUP_WIDTH
    length = block * seq_count
    tiles = length // TILE
    rows = tiles * GROUP_WIDTH
    layer_rows = rows // LAYERS
    blocks = length // block
    vmem = pl.BlockSpec(memory_space=pltpu.VMEM)
    hbm = pl.BlockSpec(memory_space=pltpu.HBM)
    single = pltpu.SemaphoreType.DMA((1,))
    by_group = pltpu.SemaphoreType.DMA((groups,))
    by_layer = pltpu.SemaphoreType.DMA((LAYERS,))
    flat = pltpu.VMEM((chan_rows, block), jnp.bfloat16)
    layered = pltpu.VMEM((groups, layer_rows, TILE), jnp.bfloat16)
    small = pltpu.VMEM((crew, groups, block), jnp.float32)
    outs = (
        jax.ShapeDtypeStruct((chan_rows, block), jnp.bfloat16),
        jax.ShapeDtypeStruct((chan_rows, block), jnp.bfloat16),
        jax.ShapeDtypeStruct(filters.shape, jnp.float32),
    )
    results = pl.pallas_call(
        functools.partial(layered_kernel, seq_count, chan_count),
        out_shape=outs,
        in_specs=[hbm] * 4,
        out_specs=(vmem, vmem, vmem),
        scratch_shapes=[
            flat,
            flat,
            pltpu.VMEM(filters.shape, jnp.float32),
            small,
            small,
            pltpu.VMEM((LAYERS, peers // 2, 2 * groups, block), jnp.bfloat16),
            pltpu.VMEM((LAYERS, peers, groups, block), jnp.float32),
            flat,
            pltpu.VMEM((groups, rows, TILE), jnp.bfloat16),
            pltpu.VMEM((groups, rows, TILE), jnp.bfloat16),
            pltpu.VMEM((blocks, block, block), jnp.bfloat16),
            pltpu.VMEM((rows, TILE), jnp.float32),
            pltpu.VMEM((rows, TILE), jnp.float32),
            layered,
            layered,
            flat,
            layered,
            pltpu.VMEM((blocks, groups, block), jnp.float32),
            pltpu.VMEM((LAYERS, crew, groups, block), jnp.float32),
            pltpu.SemaphoreType.DMA((3,)),
            single,
            single,
            single,
            single,
            single,
            single,
            pltpu.SemaphoreType.DMA((3,)),
            single,
            by_group,
            by_group,
            single,
            single,
            pltpu.SemaphoreType.DMA((groups, LAYERS)),
            pltpu.SemaphoreType.DMA((groups, LAYERS)),
            by_layer,
            single,
            by_layer,
            pltpu.SemaphoreType.REGULAR((LAYERS,)),
        ],
        compiler_params=pltpu.CompilerParams(
            collective_id=0, has_side_effects=True, vmem_limit_bytes=VMEM_LIMIT
        ),
    )(inputs, gating, grad_out, filters)
    return pl.pallas_call(
        store_kernel,
        out_shape=outs,
        in_specs=[vmem] * 3,
        out_specs=(hbm, hbm, hbm),
        scratch_shapes=[pltpu.SemaphoreType.DMA((3,))],
        compiler_params=pltpu.CompilerParams(vmem_limit_bytes=1024 * 1024),
    )(*results)


VMEM_LIMIT = 53900 * 1024


def solution(mesh):
    placed = (P("chan", "seq"), P("chan", "seq"), P("chan", "seq"), P(None, ("seq", "chan")))
    layered = mesh.shape["seq"] == 16 and mesh.shape["chan"] == 2
    return jax.shard_map(
        layered_shards if layered else shards,
        mesh=mesh,
        in_specs=placed,
        out_specs=(P("chan", "seq"), P("chan", "seq"), P(None, ("seq", "chan"))),
        check_vma=False,
    )
```
